32 devices in a mesh: clips: 2 (over x), ulysses: 4 (over y, core), tm: 4 (over z).
Axes of the slice: x: 2, y: 2, z: 4, core: 2. Of those that a mesh axis runs over, the one named last changes fastest.
Arguments:
- queries: bfloat16 [4096, 3072], P(('clips', 'tm', 'ulysses')), parts along dimension 0, may hold values from -90 to 90
- key_vectors: bfloat16 [4096, 3072], P(('clips', 'tm', 'ulysses')), parts along dimension 0, may hold values from -5 to 5
- value_vectors: bfloat16 [4096, 3072], P(('clips', 'tm', 'ulysses')), parts along dimension 0, may hold values from -6 to 6
- grad_out: bfloat16 [4096, 3072], P(('clips', 'tm', 'ulysses')), parts along dimension 0, may hold values from -6 to 6
- key_tiles: int32 [64, 3], P('clips'), parts along dimension 0, may hold values from 0 to 31, as said below
- tile_counts: int32 [64], P('clips'), parts along dimension 0, may hold values from 2 to 3, as said below
Outputs:
- attended: bfloat16 [4096, 3072], P(('clips', 'tm', 'ulysses')), parts along dimension 0
- grad_queries: bfloat16 [4096, 3072], P(('clips', 'tm', 'ulysses')), parts along dimension 0
- grad_keys: bfloat16 [4096, 3072], P(('clips', 'tm', 'ulysses')), parts along dimension 0
- grad_values: bfloat16 [4096, 3072], P(('clips', 'tm', 'ulysses')), parts along dimension 0
The draws below stay inside these ranges and needn't reach their ends.
There are 2 independent parts, one for each index of `clips`. The reference program is written for one: setup_inputs(seed, part) draws one part's arguments, and reference() takes and returns one part's arrays. A program takes and returns all parts, laid end to end along the dimension named above; each array names one. Nothing has to cross between parts.
Inputs may be any that keep to these rules, and one draw needn't show every extreme that they name: `key_tiles`: row i holds distinct tiles of the frame of query tile i and of the frames just before and after it; entry 0 is tile i itself, then one tile of the frame before and one of the frame after where those frames exist, then the rest in no fixed order; entries from position tile_counts[i] on repeat entry 0. The query tiles of one frame together list exactly 1 tiles of the frame before it and exactly 1 of the frame after it, where those frames exist. `tile_counts`: the first 1 query tiles of every frame have count 3.
All inputs are finite; a program needn't handle non-finite values.
Results may differ from the reference program's by a relative error of at most 0.022.
Values may be sent and summed in bfloat16 or wider, within the bound.
A program may use at most 192 MiB of HBM per device.

```python
import jax
import jax.numpy as jnp
from jax import lax

HEADS = 48
HEAD_DIM = 64
TILE = 64
FRAMES_SLAB = 2
FRAME_TILES = 4
FRAMES = 8
TOKENS = 2048
Q_TILES = 32
REMOTE = 1
MAXK = 3
N_TM = 4


def draw_pair(key):
    base_key = jax.random.fold_in(key, 101)
    query_key, vector_key = jax.random.split(base_key, 2)
    row_width = HEADS * HEAD_DIM
    query_draw = jnp.clip(jax.random.normal(query_key, (TOKENS, row_width), jnp.float32), -4.0, 4.0)
    key_draw = jnp.clip(jax.random.normal(vector_key, (TOKENS, row_width), jnp.float32), -4.0, 4.0)
    return (query_draw.astype(jnp.bfloat16), key_draw.astype(jnp.bfloat16))


def draw_queries(key, part):
    return draw_pair(key)[0]


def draw_key_vectors(key, part):
    return draw_pair(key)[1]


def draw_lists(key):
    base_key = jax.random.fold_in(key, 202)
    earlier_key, later_key, rank_key, count_key = jax.random.split(base_key, 4)
    frame_tiles = FRAME_TILES
    remote = REMOTE
    list_width = MAXK
    tile_total = Q_TILES
    frame_total = FRAMES
    candidate_total = frame_tiles + 2 * remote

    def first_picks(sub_key):
        return jax.random.permutation(sub_key, frame_tiles)[:remote].astype(jnp.int32)
    earlier_sets = jax.vmap(first_picks)(jax.random.split(earlier_key, frame_total))
    later_sets = jax.vmap(first_picks)(jax.random.split(later_key, frame_total))
    tile_index = jnp.arange(tile_total, dtype=jnp.int32)
    frame_of = tile_index // frame_tiles
    inner_index = tile_index % frame_tiles
    spot_index = jnp.arange(frame_tiles, dtype=jnp.int32)
    local_tiles = frame_of[:, None] * frame_tiles + spot_index[None, :]
    earlier_tiles = (frame_of[:, None] - 1) * frame_tiles + earlier_sets[frame_of]
    later_tiles = (frame_of[:, None] + 1) * frame_tiles + later_sets[frame_of]
    candidates = jnp.concatenate([local_tiles, earlier_tiles, later_tiles], axis=1)
    picked = jnp.arange(remote, dtype=jnp.int32)[None, :] == (inner_index % remote)[:, None]
    has_earlier = (frame_of > 0)[:, None]
    has_later = (frame_of < frame_total - 1)[:, None]
    priority_local = jnp.where(spot_index[None, :] == inner_index[:, None], 0, 3)
    priority_earlier = jnp.where(has_earlier, jnp.where(picked, 1, 3), 4)
    priority_later = jnp.where(has_later, jnp.where(picked, 2, 3), 4)
    priority = jnp.concatenate([priority_local, priority_earlier, priority_later], axis=1).astype(jnp.int32)

    def random_rank(sub_key):
        return jax.random.permutation(sub_key, candidate_total).astype(jnp.int32)
    ranks = jax.vmap(random_rank)(jax.random.split(rank_key, tile_total))
    ordering = jnp.argsort(priority * candidate_total + ranks, axis=1)
    chosen = jnp.take_along_axis(candidates, ordering, axis=1)[:, :list_width]
    counts = jax.random.randint(count_key, (tile_total,), list_width // 2 + 1, list_width + 1)
    counts = jnp.where(inner_index < remote, list_width, counts).astype(jnp.int32)
    slot_index = jnp.arange(list_width, dtype=jnp.int32)
    chosen = jnp.where(slot_index[None, :] < counts[:, None], chosen, chosen[:, :1])
    return (chosen.astype(jnp.int32), counts)


def draw_key_tiles(key, part):
    return draw_lists(key)[0]


def draw_tile_counts(key, part):
    return draw_lists(key)[1]


def block_scale(rng, extent, pieces, smallest, largest):
    def one(dim, shards_of):
        steps = jax.random.uniform(jax.random.fold_in(jax.random.fold_in(rng, 6), dim), (shards_of,), jnp.float32, smallest / len(pieces), largest / len(pieces))
        return jnp.repeat(jnp.exp(steps), extent[dim] // shards_of).reshape((-1,) + (1,) * (len(extent) - dim - 1))

    gain = one(*pieces[0])
    for cut in pieces[1:]:
        gain = gain * one(*cut)
    return gain


def gaussian(key, shape, scale, reach, cuts=(), kind=jnp.bfloat16):
    result = jax.random.normal(key, shape, jnp.float32) * scale
    if len(cuts) > 0:
        result = block_scale(key, shape, cuts, -0.22, 0.18) * result
    return jnp.clip(result, min=-reach, max=reach).astype(kind)


def setup_inputs(seed: int = 0, part: int = 0) -> dict:
    arg_keys = jax.random.split(jax.random.key(seed), 7)
    part_splits = jax.random.split(jax.random.fold_in(arg_keys[6], part), 7)
    return {
        "queries": draw_queries(jax.random.fold_in(jax.random.fold_in(arg_keys[6], part), 71), part),
        "key_vectors": draw_key_vectors(jax.random.fold_in(jax.random.fold_in(arg_keys[6], part), 71), part),
        "value_vectors": gaussian(part_splits[2], (TOKENS, HEADS * HEAD_DIM), 1.0, 6.0, ((0, 16),)),
        "grad_out": gaussian(part_splits[3], (TOKENS, HEADS * HEAD_DIM), 1.0, 6.0, ((0, 16),)),
        "key_tiles": draw_key_tiles(jax.random.fold_in(jax.random.fold_in(arg_keys[6], part), 71), part),
        "tile_counts": draw_tile_counts(jax.random.fold_in(jax.random.fold_in(arg_keys[6], part), 71), part),
    }


def attend(query_rows, key_rows, value_rows, grad_rows, live_keys, score_scale):
    best = lax.Precision.HIGHEST
    query_full = query_rows.astype(jnp.float32)
    key_full = key_rows.astype(jnp.float32)
    value_full = value_rows.astype(jnp.float32)
    grad_full = grad_rows.astype(jnp.float32)
    scores = jnp.einsum("bqhd,bkhd->bhqk", query_full, key_full, precision=best) * score_scale
    key_mask = live_keys[:, None, None, :]
    scores = jnp.where(key_mask, scores, -jnp.inf)
    row_peak = jnp.max(scores, axis=-1, keepdims=True)
    expo_terms = jnp.where(key_mask, jnp.exp(scores - row_peak), 0.0)
    prob_full = expo_terms / jnp.sum(expo_terms, axis=-1, keepdims=True)
    prob_low = lax.optimization_barrier(prob_full.astype(jnp.bfloat16)).astype(jnp.float32)
    out_rows = jnp.einsum("bhqk,bkhd->bqhd", prob_low, value_full, precision=best).astype(jnp.bfloat16)
    row_delta = jnp.sum(grad_full * out_rows.astype(jnp.float32), axis=-1)
    grad_probs = jnp.einsum("bqhd,bkhd->bhqk", grad_full, value_full, precision=best)
    grad_scores = prob_full * (grad_probs - jnp.transpose(row_delta, (0, 2, 1))[..., None])
    grad_low = lax.optimization_barrier(grad_scores.astype(jnp.bfloat16)).astype(jnp.float32)
    grad_query_rows = (jnp.einsum("bhqk,bkhd->bqhd", grad_low, key_full, precision=best) * score_scale).astype(jnp.bfloat16)
    key_part = jnp.einsum("bhqk,bqhd->bkhd", grad_low, query_full, precision=best) * score_scale
    value_part = jnp.einsum("bhqk,bqhd->bkhd", prob_low, grad_full, precision=best)
    return out_rows, grad_query_rows, key_part, value_part


def reference(queries, key_vectors, value_vectors, grad_out, key_tiles, tile_counts):
    own_tiles = FRAMES_SLAB * FRAME_TILES
    row_width = HEADS * HEAD_DIM
    tile_shape = (Q_TILES, TILE, HEADS, HEAD_DIM)
    query_tiled = queries.reshape(tile_shape)
    key_tiled = key_vectors.reshape(tile_shape)
    value_tiled = value_vectors.reshape(tile_shape)
    grad_tiled = grad_out.reshape(tile_shape)
    score_scale = HEAD_DIM ** -0.5

    def one_slab(slab_index):
        first_tile = (slab_index * own_tiles).astype(jnp.int32)
        tile_lists = lax.dynamic_slice(key_tiles, (first_tile, jnp.int32(0)), (own_tiles, MAXK))
        counts = lax.dynamic_slice(tile_counts, (first_tile,), (own_tiles,))
        query_block = lax.dynamic_slice_in_dim(query_tiled, first_tile, own_tiles, 0)
        grad_block = lax.dynamic_slice_in_dim(grad_tiled, first_tile, own_tiles, 0)
        key_block = key_tiled[tile_lists].reshape(own_tiles, MAXK * TILE, HEADS, HEAD_DIM)
        value_block = value_tiled[tile_lists].reshape(own_tiles, MAXK * TILE, HEADS, HEAD_DIM)
        live_keys = jnp.repeat(jnp.arange(MAXK, dtype=jnp.int32)[None, :] < counts[:, None], TILE, axis=1)
        out_rows, grad_query_rows, key_part, value_part = attend(query_block, key_block, value_block, grad_block, live_keys, score_scale)
        slot_index = (tile_lists - first_tile + FRAME_TILES).astype(jnp.int32).reshape(-1)
        ext_shape = (own_tiles + 2 * FRAME_TILES, TILE, HEADS, HEAD_DIM)
        flat_shape = (own_tiles * MAXK, TILE, HEADS, HEAD_DIM)
        key_sum = jnp.zeros(ext_shape, jnp.float32).at[slot_index].add(key_part.reshape(flat_shape))
        value_sum = jnp.zeros(ext_shape, jnp.float32).at[slot_index].add(value_part.reshape(flat_shape))
        upper_start = FRAME_TILES + own_tiles
        return (out_rows, grad_query_rows,
                key_sum[FRAME_TILES:upper_start], value_sum[FRAME_TILES:upper_start],
                key_sum[:FRAME_TILES].astype(jnp.bfloat16), value_sum[:FRAME_TILES].astype(jnp.bfloat16),
                key_sum[upper_start:].astype(jnp.bfloat16), value_sum[upper_start:].astype(jnp.bfloat16))

    results = lax.map(one_slab, jnp.arange(N_TM, dtype=jnp.int32))
    out_all, grad_query_all, key_own, value_own, key_low, value_low, key_high, value_high = results

    def combine(own_sum, lower_border, upper_border):
        lower_border = lax.optimization_barrier(lower_border).astype(jnp.float32)
        upper_border = lax.optimization_barrier(upper_border).astype(jnp.float32)
        from_above = jnp.concatenate([lower_border[1:], jnp.zeros_like(lower_border[:1])], axis=0)
        from_below = jnp.concatenate([jnp.zeros_like(upper_border[:1]), upper_border[:-1]], axis=0)
        own_sum = own_sum.at[:, own_tiles - FRAME_TILES:].add(from_above)
        own_sum = own_sum.at[:, :FRAME_TILES].add(from_below)
        return own_sum.astype(jnp.bfloat16).reshape(TOKENS, row_width)

    attended = out_all.reshape(TOKENS, row_width)
    grad_queries = grad_query_all.reshape(TOKENS, row_width)
    grad_keys = combine(key_own, key_low, key_high)
    grad_values = combine(value_own, value_low, value_high)
    return attended, grad_queries, grad_keys, grad_values
```

```python
import functools

import jax
import jax.numpy as jnp
from jax import lax
from jax.experimental import pallas as pl
from jax.experimental.pallas import tpu as pltpu
from jax.sharding import PartitionSpec as P

HEAD_DIM = 64
TILE = 64
FRAMES_SLAB = 2
LANES = 128
DEAD = -1e30
BLOCK_LIMIT = 384 * 512
CHUNK_HEADS = 6
MESH = pl.DeviceIdType.MESH
BF16 = jnp.bfloat16
F32 = jnp.float32


def position(group):
    place = lax.axis_index("ulysses")
    frame = lax.axis_index("tm") * FRAMES_SLAB + place // group
    return frame, place % group, place - place % group


def frame_device(frame, group, member):
    return {
        "tm": frame // FRAMES_SLAB,
        "ulysses": (frame % FRAMES_SLAB) * group + member,
    }


def greet(group, frames):
    frame, member, base = position(group)
    barrier = pltpu.get_barrier_semaphore()
    for step in range(1, group):
        peer = base + (member + step) % group
        pl.semaphore_signal(barrier, inc=1, device_id={"ulysses": peer}, device_id_type=MESH)

    neighbours = ((frame > 0, -1), (frame < frames - 1, 1))
    for exists, step in neighbours:
        @pl.when(exists)
        def _():
            pl.semaphore_signal(
                barrier, inc=1, device_id=frame_device(frame + step, group, member),
                device_id_type=MESH,
            )

    near = jnp.where(frame > 0, 1, 0) + jnp.where(frame < frames - 1, 1, 0)
    pl.semaphore_wait(barrier, group - 1 + near)


def remote(source, target, send, receive, device):
    return pltpu.make_async_remote_copy(
        src_ref=source, dst_ref=target, send_sem=send, recv_sem=receive,
        device_id=device, device_id_type=MESH,
    )


def heads_math(query, grad, keys, values, bias):
    scale = HEAD_DIM ** (-0.5)
    lanes = lax.broadcasted_iota(jnp.int32, query.shape, 1)
    first = lanes < HEAD_DIM
    nothing = jnp.zeros_like(query)
    query = query * jnp.asarray(scale, BF16)
    queries = jnp.concatenate([jnp.where(first, query, nothing), jnp.where(first, nothing, query)])
    grads = jnp.concatenate([jnp.where(first, grad, nothing), jnp.where(first, nothing, grad)])
    rows, columns = keys.shape[0], queries.shape[0]

    def dot(left, right, dims):
        return lax.dot_general(left, right, (dims, ((), ())), preferred_element_type=F32)

    def pick(both):
        return jnp.where(first, both[: columns // 2], both[columns // 2 :])

    scores = dot(keys, queries, ((1,), (1,)))
    bias = jnp.concatenate([bias, bias], axis=1)
    scores = scores.reshape(rows // TILE, TILE, columns) + bias[:, None, :]
    scores = scores.reshape(rows, columns)
    expo = jnp.exp(scores - jnp.max(scores, axis=0, keepdims=True))
    probs = expo * (1.0 / jnp.sum(expo, axis=0, keepdims=True))
    probs_low = probs.astype(BF16)
    grad_probs = dot(values, grads, ((1,), (1,)))
    delta = jnp.sum(probs * grad_probs, axis=0, keepdims=True)
    grad_low = (probs * (grad_probs - delta)).astype(BF16)
    attended = pick(dot(probs_low, values, ((0,), (0,)))).astype(BF16)
    grad_query = (pick(dot(grad_low, keys, ((0,), (0,)))) * scale).astype(BF16)
    key_part = dot(grad_low, queries, ((1,), (0,)))
    value_part = dot(probs_low, grads, ((1,), (0,)))
    return attended, grad_query, key_part, value_part


def block_rows(frame_rows, ext_rows):
    tiles = frame_rows // TILE
    for step in range(tiles, 0, -1):
        if tiles % step == 0 and 2 * step * TILE * ext_rows <= BLOCK_LIMIT:
            return step * TILE
    return TILE


def listing(tiles, counts, reader, source, frame_tiles, frames):
    reader = jnp.clip(reader, 0, frames - 1)
    masks = []
    for row in range(frame_tiles):
        tile = reader * frame_tiles + row
        mask = jnp.int32(0)
        for slot in range(tiles.shape[0]):
            inside = tiles[slot, tile] - source * frame_tiles
            good = (inside >= 0) & (inside < frame_tiles) & (slot < counts[tile])
            bit = lax.shift_left(jnp.int32(1), jnp.clip(inside, 0, frame_tiles - 1))
            mask = mask | jnp.where(good, bit, 0)
        masks.append(mask)
    return masks


def nth_tiles(masks, frame_tiles, count):
    union = functools.reduce(lambda left, right: left | right, masks)
    seen = jnp.int32(0)
    picked = [[] for _ in range(count)]
    for tile in range(frame_tiles):
        bit = (union >> tile) & 1
        for spot in range(count):
            picked[spot].append((bit == 1) & (seen == spot))
        seen = seen + bit
    return picked


def fused_kernel(
    group, frames, count, chunks, tiles, counts, q_in, k_in, v_in, g_in,
    out_a, out_q, out_k, out_v,
    ext, own, bias, stage, parts, result, border, landed,
    send, recv, near, halo_send, halo_recv,
    back_send, back_recv, out_send, out_recv, out_near,
):
    frame, member, base = position(group)
    rows = q_in.shape[0]
    frame_rows, chunk_width = own.shape[2], own.shape[3]
    width = chunk_width * chunks
    edge = count * TILE
    frame_tiles = frame_rows // TILE
    has_low, has_high = frame > 0, frame < frames - 1

    def lanes_of(which, chunk):
        return pl.ds(pl.multiple_of(which * width + chunk * chunk_width, LANES), chunk_width)

    def rows_of(which, start=0):
        return pl.ds(pl.multiple_of(which * rows + start, TILE), rows)

    sources = (k_in, v_in, q_in, g_in)

    def landing(number, chunk):
        if number < 2:
            return ext.at[number, chunk, rows_of(member, edge)]
        return own.at[number - 2, chunk, rows_of(member)]

    order = [(number, chunk) for chunk in range(chunks) for number in (0, 1)]
    order += [(number, chunk) for chunk in range(chunks) for number in (2, 3)]
    arriving = {}
    for number, chunk in order:
        copy = pltpu.make_async_copy(
            sources[number].at[:, lanes_of(member, chunk)], landing(number, chunk),
            near.at[number, chunk],
        )
        copy.start()
        arriving[number, chunk] = [copy]
    greet(group, frames)
    for number, chunk in order:
        for step in range(1, group):
            peer = (member + step) % group
            copy = remote(
                sources[number].at[:, lanes_of(peer, chunk)], landing(number, chunk),
                send.at[number, chunk, step - 1], recv.at[number, chunk, step - 1],
                {"ulysses": base + peer},
            )
            copy.start()
            arriving[number, chunk].append(copy)

    up_picks = nth_tiles(
        listing(tiles, counts, frame + 1, frame, frame_tiles, frames), frame_tiles, count
    )
    down_picks = nth_tiles(
        listing(tiles, counts, frame - 1, frame, frame_tiles, frames), frame_tiles, count
    )
    picks = (up_picks, down_picks)

    halo_rows = (pl.ds(0, edge), pl.ds(edge + frame_rows, edge))

    def halo_copy(number, way, chunk, target):
        return remote(
            stage.at[number, way, chunk], ext.at[number, chunk, halo_rows[way]],
            halo_send.at[number, way, chunk], halo_recv.at[number, way, chunk],
            frame_device(target, group, member),
        )

    def back_copy(number, way, chunk, target):
        return remote(
            border.at[number, way, chunk], landed.at[number, way, chunk],
            back_send.at[number, way, chunk], back_recv.at[number, way, chunk],
            frame_device(target, group, member),
        )

    for way, exists in enumerate((has_low, has_high)):
        @pl.when(jnp.logical_not(exists))
        def _():
            for number in range(2):
                for chunk in range(chunks):
                    ext[number, chunk, halo_rows[way]] = jnp.zeros((edge, chunk_width), BF16)
                    landed[number, 1 - way, chunk] = jnp.zeros((edge, chunk_width), BF16)

    for chunk in range(chunks):
        for number in range(2):
            for copy in arriving[number, chunk]:
                copy.wait()
            for way in range(2):
                for spot in range(count):
                    chosen = ext[number, chunk, pl.ds(edge, TILE)]
                    for tile in range(1, frame_tiles):
                        here = ext[number, chunk, pl.ds(edge + tile * TILE, TILE)]
                        chosen = jnp.where(picks[way][spot][tile], here, chosen)
                    stage[number, way, chunk, pl.ds(spot * TILE, TILE)] = chosen
        for way, exists in enumerate((has_high, has_low)):
            @pl.when(exists)
            def _():
                for number in range(2):
                    halo_copy(number, way, chunk, frame + (1 if way == 0 else -1)).start()

    blocks, step_rows = bias.shape[0], bias.shape[2]
    low_rows = listing(tiles, counts, frame, frame - 1, frame_tiles, frames)
    own_masks = listing(tiles, counts, frame, frame, frame_tiles, frames)
    high_rows = listing(tiles, counts, frame, frame + 1, frame_tiles, frames)

    def edge_hits(masks):
        picked = nth_tiles(masks, frame_tiles, count)
        hits = []
        for spot in range(count):
            bit = jnp.int32(0)
            for tile in range(frame_tiles):
                bit = bit + jnp.where(picked[spot][tile], 1 << tile, 0)
            hits.append([(mask & bit) != 0 for mask in masks])
        return hits

    hits = edge_hits(low_rows)
    hits += [[((mask >> tile) & 1) == 1 for mask in own_masks] for tile in range(frame_tiles)]
    hits += edge_hits(high_rows)
    block_tiles = step_rows // TILE
    inner = lax.broadcasted_iota(jnp.int32, (1, step_rows), 1) // TILE
    for number, row in enumerate(hits):
        for block in range(blocks):
            line = jnp.full((1, step_rows), DEAD, F32)
            for spot in range(block_tiles):
                level = jnp.where(row[block * block_tiles + spot], 0.0, DEAD)
                line = jnp.where(inner == spot, level, line)
            bias[block, pl.ds(number, 1)] = line

    leaving = []

    def share(number, chunk):
        target = (out_a, out_q, out_k, out_v)[number]
        columns = lanes_of(member, chunk)
        copy = pltpu.make_async_copy(
            result.at[number, chunk, rows_of(member)], target.at[:, columns],
            out_near.at[number, chunk],
        )
        copy.start()
        leaving.append(copy)
        for step in range(1, group):
            peer = (member + step) % group
            copy = remote(
                result.at[number, chunk, rows_of(peer)], target.at[:, columns],
                out_send.at[number, chunk, step - 1], out_recv.at[number, chunk, step - 1],
                {"ulysses": base + peer},
            )
            copy.start()
            leaving.append(copy)

    for chunk in range(chunks):
        for number in (2, 3):
            for copy in arriving[number, chunk]:
                copy.wait()
        for way, comes in enumerate((has_low, has_high)):
            @pl.when(comes)
            def _():
                for number in range(2):
                    halo_copy(number, way, chunk, frame).wait_recv()

        @pl.loop(0, chunk_width // LANES)
        def _(pair):
            lanes = pl.ds(pl.multiple_of(pair * LANES, LANES), LANES)
            for block in range(blocks):
                span = pl.ds(block * step_rows, step_rows)
                out, grad_rows, key_part, value_part = heads_math(
                    own[0, chunk, span, lanes], own[1, chunk, span, lanes],
                    ext[0, chunk, :, lanes], ext[1, chunk, :, lanes], bias[block],
                )
                result[0, chunk, span, lanes] = out
                result[1, chunk, span, lanes] = grad_rows
                for number, part in enumerate((key_part, value_part)):
                    if block:
                        part = part + parts[number, chunk, :, lanes]
                    parts[number, chunk, :, lanes] = part

        for number in range(2):
            for way in range(2):
                border[number, way, chunk] = parts[number, chunk, halo_rows[way]].astype(BF16)
        for way, goes in enumerate((has_low, has_high)):
            @pl.when(goes)
            def _():
                for number in range(2):
                    back_copy(number, way, chunk, frame + (1 if way else -1)).start()
        share(0, chunk)
        share(1, chunk)

    for chunk in range(chunks):
        for way, comes in enumerate((has_high, has_low)):
            @pl.when(comes)
            def _():
                for number in range(2):
                    back_copy(number, way, chunk, frame).wait_recv()
        for number in range(2):
            for tile in range(frame_tiles):
                total = parts[number, chunk, pl.ds(edge + tile * TILE, TILE)]
                for way in range(2):
                    for spot in range(count):
                        part = landed[number, way, chunk, pl.ds(spot * TILE, TILE)].astype(F32)
                        total = total + jnp.where(picks[way][spot][tile], part, 0.0)
                result[2 + number, chunk, pl.ds(tile * TILE, TILE)] = total.astype(BF16)
            share(2 + number, chunk)

    for way, (halo_goes, back_goes) in enumerate(((has_high, has_low), (has_low, has_high))):
        @pl.when(halo_goes)
        def _():
            for chunk in range(chunks):
                for number in range(2):
                    halo_copy(number, way, chunk, frame).wait_send()

        @pl.when(back_goes)
        def _():
            for chunk in range(chunks):
                for number in range(2):
                    back_copy(number, way, chunk, frame).wait_send()
    for copy in leaving:
        copy.wait()


def flush_kernel(*refs):
    sems = refs[8]
    copies = [pltpu.make_async_copy(refs[n], refs[4 + n], sems.at[n]) for n in range(4)]
    for copy in copies:
        copy.start()
    for copy in copies:
        copy.wait()


def per_device(frames, group, queries, key_vectors, value_vectors, grad_out, key_tiles, tile_counts):
    rows, columns = queries.shape
    width = columns // group
    frame_rows = rows * group
    frame_tiles = frame_rows // TILE
    count = max(1, frame_tiles // 8)
    edge = count * TILE
    ext_rows = frame_rows + 2 * edge
    chunk_width = CHUNK_HEADS * HEAD_DIM
    if width % chunk_width:
        chunk_width = LANES
    chunks = width // chunk_width
    step_rows = block_rows(frame_rows, ext_rows)

    smem = pl.BlockSpec(memory_space=pltpu.SMEM)
    vmem = pl.BlockSpec(memory_space=pltpu.VMEM)
    hbm = pl.BlockSpec(memory_space=pltpu.HBM)
    dma = pltpu.SemaphoreType.DMA
    own_shape = jax.ShapeDtypeStruct((rows, columns), BF16)
    arguments = [
        pltpu.with_memory_space_constraint(value, pltpu.HBM)
        for value in (key_tiles.T, tile_counts, queries, key_vectors, value_vectors, grad_out)
    ]
    results = pl.pallas_call(
        functools.partial(fused_kernel, group, frames, count, chunks),
        out_shape=(own_shape,) * 4,
        in_specs=[smem, smem] + [hbm] * 4,
        out_specs=(vmem,) * 4,
        scratch_shapes=[
            pltpu.VMEM((2, chunks, ext_rows, chunk_width), BF16),
            pltpu.VMEM((2, chunks, frame_rows, chunk_width), BF16),
            pltpu.VMEM((frame_rows // step_rows, ext_rows // TILE, step_rows), F32),
            pltpu.VMEM((2, 2, chunks, edge, chunk_width), BF16),
            pltpu.VMEM((2, chunks, ext_rows, chunk_width), F32),
            pltpu.VMEM((4, chunks, frame_rows, chunk_width), BF16),
            pltpu.VMEM((2, 2, chunks, edge, chunk_width), BF16),
            pltpu.VMEM((2, 2, chunks, edge, chunk_width), BF16),
            dma((4, chunks, group - 1)), dma((4, chunks, group - 1)), dma((4, chunks)),
            dma((2, 2, chunks)), dma((2, 2, chunks)), dma((2, 2, chunks)), dma((2, 2, chunks)),
            dma((4, chunks, group - 1)), dma((4, chunks, group - 1)), dma((4, chunks)),
        ],
        compiler_params=pltpu.CompilerParams(
            collective_id=0, has_side_effects=True, vmem_limit_bytes=32 << 20
        ),
        name="frame_attention",
    )(*arguments)
    return pl.pallas_call(
        flush_kernel,
        out_shape=(own_shape,) * 4,
        in_specs=[vmem] * 4,
        out_specs=(hbm,) * 4,
        scratch_shapes=[dma((4,))],
        compiler_params=pltpu.CompilerParams(vmem_limit_bytes=16 << 20),
        name="flush_results",
    )(*results)


def solution(mesh):
    tokens = P(("clips", "tm", "ulysses"), None)
    group = mesh.shape["ulysses"] // FRAMES_SLAB
    frames = mesh.shape["tm"] * FRAMES_SLAB
    return jax.shard_map(
        functools.partial(per_device, frames, group),
        mesh=mesh,
        in_specs=(tokens, tokens, tokens, tokens, P("clips", None), P("clips")),
        out_specs=(tokens,) * 4,
        check_vma=False,
    )
```

```python
import functools

import jax
import jax.numpy as jnp
from jax import lax
from jax.experimental import pallas as pl
from jax.experimental.pallas import tpu as pltpu
from jax.sharding import PartitionSpec as P

HEAD_DIM = 64
TILE = 64
FRAMES_SLAB = 2
LANES = 128
DEAD = -1e30
BLOCK_LIMIT = 384 * 512
CHUNK = 256
LAG = 1
MESH = pl.DeviceIdType.MESH
BF16 = jnp.bfloat16
F32 = jnp.float32


def remote(source, target, send, receive, device):
    return pltpu.make_async_remote_copy(
        src_ref=source, dst_ref=target, send_sem=send, recv_sem=receive,
        device_id=device, device_id_type=MESH,
    )


def heads_math(query, grad, keys, values, bias):
    scale = HEAD_DIM ** (-0.5)
    lanes = lax.broadcasted_iota(jnp.int32, query.shape, 1)
    first = lanes < HEAD_DIM
    nothing = jnp.zeros_like(query)
    query = query * jnp.asarray(scale, BF16)
    queries = jnp.concatenate([jnp.where(first, query, nothing), jnp.where(first, nothing, query)])
    grads = jnp.concatenate([jnp.where(first, grad, nothing), jnp.where(first, nothing, grad)])
    rows, columns = keys.shape[0], queries.shape[0]

    def dot(left, right, dims):
        return lax.dot_general(left, right, (dims, ((), ())), preferred_element_type=F32)

    def pick(both):
        return jnp.where(first, both[: columns // 2], both[columns // 2 :])

    scores = dot(keys, queries, ((1,), (1,)))
    bias = jnp.concatenate([bias, bias], axis=1)
    scores = scores.reshape(rows // TILE, TILE, columns) + bias[:, None, :]
    scores = scores.reshape(rows, columns)
    expo = jnp.exp(scores - jnp.max(scores, axis=0, keepdims=True))
    probs = expo * (1.0 / jnp.sum(expo, axis=0, keepdims=True))
    probs_low = probs.astype(BF16)
    grad_probs = dot(values, grads, ((1,), (1,)))
    delta = jnp.sum(probs * grad_probs, axis=0, keepdims=True)
    grad_low = (probs * (grad_probs - delta)).astype(BF16)
    attended = pick(dot(probs_low, values, ((0,), (0,)))).astype(BF16)
    grad_query = (pick(dot(grad_low, keys, ((0,), (0,)))) * scale).astype(BF16)
    key_part = dot(grad_low, queries, ((1,), (0,)))
    value_part = dot(probs_low, grads, ((1,), (0,)))
    return attended, grad_query, key_part, value_part


def block_rows(frame_rows, ext_rows):
    tiles = frame_rows // TILE
    for step in range(tiles, 0, -1):
        if tiles % step == 0 and 2 * step * TILE * ext_rows <= BLOCK_LIMIT:
            return step * TILE
    return TILE


def listing(tiles, counts, reader, source, frame_tiles, frames):
    reader = jnp.clip(reader, 0, frames - 1)
    masks = []
    for row in range(frame_tiles):
        tile = reader * frame_tiles + row
        mask = jnp.int32(0)
        for slot in range(tiles.shape[0]):
            inside = tiles[slot, tile] - source * frame_tiles
            good = (inside >= 0) & (inside < frame_tiles) & (slot < counts[tile])
            bit = lax.shift_left(jnp.int32(1), jnp.clip(inside, 0, frame_tiles - 1))
            mask = mask | jnp.where(good, bit, 0)
        masks.append(mask)
    return masks


def nth_tiles(masks, frame_tiles, count):
    union = functools.reduce(lambda left, right: left | right, masks)
    seen = jnp.int32(0)
    picked = [[] for _ in range(count)]
    for tile in range(frame_tiles):
        bit = (union >> tile) & 1
        for spot in range(count):
            picked[spot].append((bit == 1) & (seen == spot))
        seen = seen + bit
    return picked


def forward_relayed(chunk, chunks, share, slabs):
    return ((chunk + 1) * share) // slabs > (chunk * share) // slabs


def backward_relayed(chunk, chunks, share, slabs):
    return chunk < (chunks * share + slabs - 1) // slabs


RELAYED = (forward_relayed, backward_relayed)


def cuts(chunks, first):
    spans, start, size = [], 0, first
    while start < chunks:
        stop = min(chunks, start + size)
        spans.append((start, stop))
        start, size = stop, size + 1
    return spans


def fused_kernel(
    group, slabs, count, chunks, tiles, counts, q_in, k_in, v_in, g_in,
    early, late,
    own, bias, outgoing, incoming, relay, parts, sums, result,
    send, recv, near, edge_send, edge_recv, relay_send, relay_recv,
    out_send, out_recv, out_near,
):
    place, slab = lax.axis_index("ulysses"), lax.axis_index("tm")
    side, member = place // group, place % group
    base = side * group
    frames = slabs * FRAMES_SLAB
    frame = slab * FRAMES_SLAB + side
    rows, frame_rows, width = q_in.shape[0], own.shape[1], own.shape[2]
    chunk_width = width // chunks
    edge = count * TILE
    frame_tiles = frame_rows // TILE

    turn = 2 * side - 1
    far_slab, onward_slab = slab + turn, slab - turn
    has_far = (far_slab >= 0) & (far_slab < slabs)
    has_onward = (onward_slab >= 0) & (onward_slab < slabs)
    across = {"ulysses": (1 - side) * group + member}
    far = {**across, "tm": jnp.clip(far_slab, 0, slabs - 1)}
    onward = {"tm": jnp.clip(onward_slab, 0, slabs - 1)}
    behind = {"tm": jnp.clip(far_slab, 0, slabs - 1)}
    from_end, from_start = slabs - 1 - slab, slab
    my_share = jnp.where(side == 1, from_end, from_start)
    other_share = jnp.where(side == 1, from_start, from_end)

    def lanes_of(which, start, size):
        return pl.ds(pl.multiple_of(which * width + start, LANES), size)

    def rows_of(which):
        return pl.ds(pl.multiple_of(which * rows, TILE), rows)

    sources = (k_in, v_in, q_in, g_in)
    pieces = {}
    key_cuts, query_cuts = cuts(chunks, 1), cuts(chunks, max(1, chunks // 2))

    def take(number, index, span):
        start, size = span[0] * chunk_width, (span[1] - span[0]) * chunk_width
        copy = pltpu.make_async_copy(
            sources[number].at[:, lanes_of(member, start, size)],
            own.at[number, rows_of(member), pl.ds(start, size)], near.at[number, index],
        )
        copy.start()
        pieces[number, index] = [copy]

    def trade(number, index, span):
        start, size = span[0] * chunk_width, (span[1] - span[0]) * chunk_width
        for step in range(1, group):
            peer = (member + step) % group
            copy = remote(
                sources[number].at[:, lanes_of(peer, start, size)],
                own.at[number, rows_of(member), pl.ds(start, size)],
                send.at[number, index, step - 1], recv.at[number, index, step - 1],
                {"ulysses": base + peer},
            )
            copy.start()
            pieces[number, index].append(copy)

    for index, span in enumerate(key_cuts):
        for number in (0, 1):
            take(number, index, span)

    barrier = pltpu.get_barrier_semaphore()

    def hail(device):
        pl.semaphore_signal(barrier, inc=1, device_id=device, device_id_type=MESH)

    for step in range(1, group):
        hail({"ulysses": base + (member + step) % group})
    hail(across)

    @pl.when(has_far)
    def _():
        hail(far)
        hail(behind)

    @pl.when(has_onward)
    def _():
        hail(onward)

    across_frame, far_frame = frame - turn, frame + turn
    picks = [
        nth_tiles(listing(tiles, counts, reader, frame, frame_tiles, frames), frame_tiles, count)
        for reader in (across_frame, far_frame)
    ]
    pl.semaphore_wait(
        barrier, group + jnp.where(has_far, 2, 0) + jnp.where(has_onward, 1, 0)
    )
    for index, span in enumerate(key_cuts):
        for number in (0, 1):
            trade(number, index, span)

    def edge_copy(phase, way, chunk, device):
        return remote(
            outgoing.at[phase, way, chunk], incoming.at[phase, way, chunk],
            edge_send.at[phase, way, chunk], edge_recv.at[phase, way, chunk], device,
        )

    def relay_in(phase, chunk):
        return remote(
            outgoing.at[phase, 1, chunk], relay.at[phase, chunk],
            edge_send.at[phase, 1, chunk], relay_recv.at[phase, chunk], across,
        )

    def relay_out(phase, chunk):
        return remote(
            relay.at[phase, chunk], incoming.at[phase, 1, chunk],
            relay_send.at[phase, chunk], edge_recv.at[phase, 1, chunk], onward,
        )

    def passes(phase, chunk):
        return has_onward & RELAYED[phase](chunk, chunks, other_share, slabs)

    def send_edges(phase, chunk):
        edge_copy(phase, 0, chunk, across).start()
        relayed = RELAYED[phase](chunk, chunks, my_share, slabs)

        @pl.when(has_far & jnp.logical_not(relayed))
        def _():
            edge_copy(phase, 1, chunk, far).start()

        @pl.when(has_far & relayed)
        def _():
            relay_in(phase, chunk).start()

    def pass_on(phase, chunk):
        @pl.when(passes(phase, chunk))
        def _():
            relay_in(phase, chunk).wait_recv()
            relay_out(phase, chunk).start()

    def receive_edges(phase, chunk):
        edge_copy(phase, 0, chunk, across).wait_recv()

        @pl.when(has_far)
        def _():
            edge_copy(phase, 1, chunk, far).wait_recv()

    def settle_edges(phase, chunk):
        edge_copy(phase, 0, chunk, across).wait_send()

        @pl.when(has_far)
        def _():
            edge_copy(phase, 1, chunk, far).wait_send()

        @pl.when(passes(phase, chunk))
        def _():
            relay_out(phase, chunk).wait_send()

    for index, span in enumerate(key_cuts):
        for number in (0, 1):
            for copy in pieces[number, index]:
                copy.wait()
        for chunk in range(*span):
            columns = pl.ds(chunk * chunk_width, chunk_width)
            for number in (0, 1):
                for way in range(2):
                    for spot in range(count):
                        chosen = own[number, pl.ds(0, TILE), columns]
                        for tile in range(1, frame_tiles):
                            here = own[number, pl.ds(tile * TILE, TILE), columns]
                            chosen = jnp.where(picks[way][spot][tile], here, chosen)
                        outgoing[0, way, chunk, number, pl.ds(spot * TILE, TILE)] = chosen
            send_edges(0, chunk)
        if index == 0:
            for piece, part in enumerate(query_cuts):
                for number in (2, 3):
                    take(number, piece, part)
                    trade(number, piece, part)

    @pl.when(jnp.logical_not(has_far))
    def _():
        for phase in range(2):
            for chunk in range(chunks):
                incoming[phase, 1, chunk] = jnp.zeros((2, edge, chunk_width), BF16)

    blocks, step_rows = bias.shape[0], bias.shape[2]
    across_rows = listing(tiles, counts, frame, across_frame, frame_tiles, frames)
    own_masks = listing(tiles, counts, frame, frame, frame_tiles, frames)
    far_rows = listing(tiles, counts, frame, far_frame, frame_tiles, frames)

    def edge_hits(masks):
        picked = nth_tiles(masks, frame_tiles, count)
        hits = []
        for spot in range(count):
            bit = jnp.int32(0)
            for tile in range(frame_tiles):
                bit = bit + jnp.where(picked[spot][tile], 1 << tile, 0)
            hits.append([(mask & bit) != 0 for mask in masks])
        return hits

    hits = edge_hits(across_rows)
    hits += [[((mask >> tile) & 1) == 1 for mask in own_masks] for tile in range(frame_tiles)]
    hits += edge_hits(far_rows)
    block_tiles = step_rows // TILE
    inner = lax.broadcasted_iota(jnp.int32, (1, step_rows), 1) // TILE
    for number, row in enumerate(hits):
        for block in range(blocks):
            line = jnp.full((1, step_rows), DEAD, F32)
            for spot in range(block_tiles):
                level = jnp.where(row[block * block_tiles + spot], 0.0, DEAD)
                line = jnp.where(inner == spot, level, line)
            bias[block, pl.ds(number, 1)] = line

    leaving = {}

    def share(phase, chunk):
        start = chunk * chunk_width
        target, columns = (early, late)[phase], pl.ds(start, chunk_width)
        there = lanes_of(member, start, chunk_width)
        copies = [pltpu.make_async_copy(
            result.at[phase, :, rows_of(member), columns], target.at[:, :, there],
            out_near.at[phase, chunk],
        )]
        for step in range(1, group):
            peer = (member + step) % group
            copies.append(remote(
                result.at[phase, :, rows_of(peer), columns], target.at[:, :, there],
                out_send.at[phase, chunk, step - 1], out_recv.at[phase, chunk, step - 1],
                {"ulysses": base + peer},
            ))
        for copy in copies:
            copy.start()
        leaving[phase, chunk] = copies

    def attend(chunk):
        @pl.loop(0, chunk_width // LANES)
        def _(pair):
            inside = pl.ds(pl.multiple_of(pair * LANES, LANES), LANES)
            lanes = pl.ds(pl.multiple_of(chunk * chunk_width + pair * LANES, LANES), LANES)

            def stacked(number):
                return jnp.concatenate([
                    incoming[0, 0, chunk, number, :, inside], own[number, :, lanes],
                    incoming[0, 1, chunk, number, :, inside],
                ])

            for block in range(blocks):
                span = pl.ds(block * step_rows, step_rows)
                out, grad_rows, key_part, value_part = heads_math(
                    own[2, span, lanes], own[3, span, lanes], stacked(0), stacked(1), bias[block],
                )
                result[0, 0, span, lanes] = out
                result[0, 1, span, lanes] = grad_rows
                for number, part in enumerate((key_part, value_part)):
                    if block:
                        part = part + sums[number]
                    if block + 1 < blocks:
                        sums[number] = part
                        continue
                    outgoing[1, 0, chunk, number, :, inside] = part[:edge].astype(BF16)
                    parts[number, :, lanes] = part[edge : edge + frame_rows]
                    outgoing[1, 1, chunk, number, :, inside] = part[edge + frame_rows :].astype(BF16)

    for chunk in range(chunks + LAG):
        if chunk < chunks:
            pass_on(0, chunk)
        ready = chunk - LAG
        if ready < 0:
            continue
        for piece, part in enumerate(query_cuts):
            if part[0] == ready:
                for number in (2, 3):
                    for copy in pieces[number, piece]:
                        copy.wait()
        receive_edges(0, ready)
        attend(ready)
        send_edges(1, ready)
        share(0, ready)

    for chunk in range(chunks):
        settle_edges(0, chunk)

    def gather(chunk):
        columns = pl.ds(chunk * chunk_width, chunk_width)
        for number in range(2):
            for tile in range(frame_tiles):
                span = pl.ds(tile * TILE, TILE)
                total = parts[number, span, columns]
                for way in range(2):
                    for spot in range(count):
                        part = incoming[1, way, chunk, number, pl.ds(spot * TILE, TILE)].astype(F32)
                        total = total + jnp.where(picks[way][spot][tile], part, 0.0)
                result[1, number, span, columns] = total.astype(BF16)
        share(1, chunk)

    for chunk in range(chunks + LAG):
        if chunk < chunks:
            pass_on(1, chunk)
        ready = chunk - LAG
        if ready < 0:
            continue
        for copy in leaving.pop((0, ready)):
            copy.wait()
        receive_edges(1, ready)
        gather(ready)

    for chunk in range(chunks):
        settle_edges(1, chunk)
        for copy in leaving.pop((1, chunk)):
            copy.wait()


def flush_kernel(early, late, *refs):
    sems = refs[4]
    copies = [
        pltpu.make_async_copy((early, late)[n // 2].at[n % 2], refs[n], sems.at[n])
        for n in range(4)
    ]
    for copy in copies:
        copy.start()
    for copy in copies:
        copy.wait()


def per_device(slabs, group, queries, key_vectors, value_vectors, grad_out, key_tiles, tile_counts):
    rows, columns = queries.shape
    width = columns // group
    frame_rows = rows * group
    frame_tiles = frame_rows // TILE
    count = max(1, frame_tiles // 8)
    edge = count * TILE
    ext_rows = frame_rows + 2 * edge
    chunk_width = LANES if width % CHUNK else CHUNK
    chunks = width // chunk_width
    step_rows = block_rows(frame_rows, ext_rows)
    blocks = frame_rows // step_rows
    key_pieces, query_pieces = len(cuts(chunks, 1)), len(cuts(chunks, max(1, chunks // 2)))
    most = max(key_pieces, query_pieces)

    smem = pl.BlockSpec(memory_space=pltpu.SMEM)
    vmem = pl.BlockSpec(memory_space=pltpu.VMEM)
    hbm = pl.BlockSpec(memory_space=pltpu.HBM)
    dma = pltpu.SemaphoreType.DMA
    arguments = [
        pltpu.with_memory_space_constraint(value, pltpu.HBM)
        for value in (key_tiles.T, tile_counts, queries, key_vectors, value_vectors, grad_out)
    ]
    results = pl.pallas_call(
        functools.partial(fused_kernel, group, slabs, count, chunks),
        out_shape=(jax.ShapeDtypeStruct((2, rows, columns), BF16),) * 2,
        in_specs=[smem, smem] + [hbm] * 4,
        out_specs=(vmem,) * 2,
        scratch_shapes=[
            pltpu.VMEM((4, frame_rows, width), BF16),
            pltpu.VMEM((blocks, ext_rows // TILE, step_rows), F32),
            pltpu.VMEM((2, 2, chunks, 2, edge, chunk_width), BF16),
            pltpu.VMEM((2, 2, chunks, 2, edge, chunk_width), BF16),
            pltpu.VMEM((2, chunks, 2, edge, chunk_width), BF16),
            pltpu.VMEM((2, frame_rows, width), F32),
            pltpu.VMEM((2, ext_rows if blocks > 1 else TILE, LANES), F32),
            pltpu.VMEM((2, 2, frame_rows, width), BF16),
            dma((4, most, group - 1)), dma((4, most, group - 1)), dma((4, most)),
            dma((2, 2, chunks)), dma((2, 2, chunks)), dma((2, chunks)), dma((2, chunks)),
            dma((2, chunks, group - 1)), dma((2, chunks, group - 1)), dma((2, chunks)),
        ],
        compiler_params=pltpu.CompilerParams(
            collective_id=0, has_side_effects=True, vmem_limit_bytes=32 << 20
        ),
        name="frame_attention",
    )(*arguments)
    return pl.pallas_call(
        flush_kernel,
        out_shape=(jax.ShapeDtypeStruct((rows, columns), BF16),) * 4,
        in_specs=[vmem] * 2,
        out_specs=(hbm,) * 4,
        scratch_shapes=[dma((4,))],
        compiler_params=pltpu.CompilerParams(vmem_limit_bytes=16 << 20),
        name="flush_results",
    )(*results)


def solution(mesh):
    tokens = P(("clips", "tm", "ulysses"), None)
    group = mesh.shape["ulysses"] // FRAMES_SLAB
    return jax.shard_map(
        functools.partial(per_device, mesh.shape["tm"], group),
        mesh=mesh,
        in_specs=(tokens, tokens, tokens, tokens, P("clips", None), P("clips")),
        out_specs=(tokens,) * 4,
        check_vma=False,
    )
```

```python
import functools

import jax
import jax.numpy as jnp
from jax import lax
from jax.experimental import pallas as pl
from jax.experimental.pallas import tpu as pltpu
from jax.sharding import PartitionSpec as P

HEAD_DIM = 64
TILE = 64
FRAMES_SLAB = 2
LANES = 128
DEAD = -1e30
BLOCK_LIMIT = 384 * 512
CHUNK = 256
LAG = 1
HOLD = 1
MESH = pl.DeviceIdType.MESH
BF16 = jnp.bfloat16
F32 = jnp.float32


def remote(source, target, send, receive, device):
    return pltpu.make_async_remote_copy(
        src_ref=source, dst_ref=target, send_sem=send, recv_sem=receive,
        device_id=device, device_id_type=MESH,
    )


def heads_math(query, grad, keys, values, bias):
    scale = HEAD_DIM ** (-0.5)
    lanes = lax.broadcasted_iota(jnp.int32, query.shape, 1)
    first = lanes < HEAD_DIM
    nothing = jnp.zeros_like(query)
    query = query * jnp.asarray(scale, BF16)
    queries = jnp.concatenate([jnp.where(first, query, nothing), jnp.where(first, nothing, query)])
    grads = jnp.concatenate([jnp.where(first, grad, nothing), jnp.where(first, nothing, grad)])
    rows, columns = keys.shape[0], queries.shape[0]

    def dot(left, right, dims):
        return lax.dot_general(left, right, (dims, ((), ())), preferred_element_type=F32)

    def pick(both):
        return jnp.where(first, both[: columns // 2], both[columns // 2 :])

    scores = dot(keys, queries, ((1,), (1,)))
    bias = jnp.concatenate([bias, bias], axis=1)
    scores = scores.reshape(rows // TILE, TILE, columns) + bias[:, None, :]
    scores = scores.reshape(rows, columns)
    expo = jnp.exp(scores - jnp.max(scores, axis=0, keepdims=True))
    probs = expo * (1.0 / jnp.sum(expo, axis=0, keepdims=True))
    probs_low = probs.astype(BF16)
    grad_probs = dot(values, grads, ((1,), (1,)))
    delta = jnp.sum(probs * grad_probs, axis=0, keepdims=True)
    grad_low = (probs * (grad_probs - delta)).astype(BF16)
    attended = pick(dot(probs_low, values, ((0,), (0,)))).astype(BF16)
    grad_query = (pick(dot(grad_low, keys, ((0,), (0,)))) * scale).astype(BF16)
    key_part = dot(grad_low, queries, ((1,), (0,)))
    value_part = dot(probs_low, grads, ((1,), (0,)))
    return attended, grad_query, key_part, value_part


def block_rows(frame_rows, ext_rows):
    tiles = frame_rows // TILE
    for step in range(tiles, 0, -1):
        if tiles % step == 0 and 2 * step * TILE * ext_rows <= BLOCK_LIMIT:
            return step * TILE
    return TILE


def listing(tiles, counts, reader, source, frame_tiles, frames):
    reader = jnp.clip(reader, 0, frames - 1)
    masks = []
    for row in range(frame_tiles):
        tile = reader * frame_tiles + row
        mask = jnp.int32(0)
        for slot in range(tiles.shape[0]):
            inside = tiles[slot, tile] - source * frame_tiles
            good = (inside >= 0) & (inside < frame_tiles) & (slot < counts[tile])
            bit = lax.shift_left(jnp.int32(1), jnp.clip(inside, 0, frame_tiles - 1))
            mask = mask | jnp.where(good, bit, 0)
        masks.append(mask)
    return masks


def nth_tiles(masks, frame_tiles, count):
    union = functools.reduce(lambda left, right: left | right, masks)
    seen = jnp.int32(0)
    picked = [[] for _ in range(count)]
    for tile in range(frame_tiles):
        bit = (union >> tile) & 1
        for spot in range(count):
            picked[spot].append((bit == 1) & (seen == spot))
        seen = seen + bit
    return picked


def chunk_spans(width):
    sizes = [LANES] * (width // LANES)
    if width % CHUNK == 0 and width > CHUNK:
        sizes = [LANES] + [CHUNK] * (width // CHUNK - 1) + [CHUNK - LANES]
    return [(sum(sizes[:n]), size) for n, size in enumerate(sizes)]


def relayed(phase, chunk, share, slabs, spans):
    if phase == 0 and chunk + 1 == len(spans):
        return share < 0
    if phase == 0:
        return ((chunk + 1) * share) // slabs > (chunk * share) // slabs
    start, size = spans[chunk]
    total = spans[-1][0] + spans[-1][1]
    return (start + size) * slabs <= total * share


def cuts(chunks, first):
    spans, start, size = [], 0, first
    while start < chunks:
        stop = min(chunks, start + size)
        spans.append((start, stop))
        start, size = stop, size + 1
    return spans


def fused_kernel(
    group, slabs, count, spans, tiles_in, counts_in, q_in, k_in, v_in, g_in,
    early, late,
    own, bias, outgoing, incoming, relay, parts, sums, result,
    send, recv, near, edge_send, edge_recv, relay_send, relay_recv,
    out_send, out_recv, out_near, tiles, counts, list_sem,
):
    place, slab = lax.axis_index("ulysses"), lax.axis_index("tm")
    side, member = place // group, place % group
    base = side * group
    frames = slabs * FRAMES_SLAB
    frame = slab * FRAMES_SLAB + side
    rows, frame_rows, width = q_in.shape[0], own.shape[1], own.shape[2]
    chunks, widest = len(spans), outgoing.shape[5]
    edge = count * TILE
    frame_tiles = frame_rows // TILE

    turn = 2 * side - 1
    far_slab, onward_slab = slab + turn, slab - turn
    has_far = (far_slab >= 0) & (far_slab < slabs)
    has_onward = (onward_slab >= 0) & (onward_slab < slabs)
    across = {"ulysses": (1 - side) * group + member}
    far = {**across, "tm": jnp.clip(far_slab, 0, slabs - 1)}
    onward = {"tm": jnp.clip(onward_slab, 0, slabs - 1)}
    behind = {"tm": jnp.clip(far_slab, 0, slabs - 1)}
    from_end, from_start = slabs - 1 - slab, slab
    my_share = jnp.where(side == 1, from_end, from_start)
    other_share = jnp.where(side == 1, from_start, from_end)

    def lanes_of(which, start, size):
        return pl.ds(pl.multiple_of(which * width + start, LANES), size)

    def rows_of(which):
        return pl.ds(pl.multiple_of(which * rows, TILE), rows)

    sources = (k_in, v_in, q_in, g_in)
    pieces = {}
    key_cuts, query_cuts = cuts(chunks, 1), cuts(chunks, max(1, chunks // 2))

    def take(number, index, span):
        start = spans[span[0]][0]
        size = sum(spans[span[1] - 1]) - start
        copy = pltpu.make_async_copy(
            sources[number].at[:, lanes_of(member, start, size)],
            own.at[number, rows_of(member), pl.ds(start, size)], near.at[number, index],
        )
        copy.start()
        pieces[number, index] = [copy]

    def trade(number, index, span):
        start = spans[span[0]][0]
        size = sum(spans[span[1] - 1]) - start
        for step in range(1, group):
            peer = (member + step) % group
            copy = remote(
                sources[number].at[:, lanes_of(peer, start, size)],
                own.at[number, rows_of(member), pl.ds(start, size)],
                send.at[number, index, step - 1], recv.at[number, index, step - 1],
                {"ulysses": base + peer},
            )
            copy.start()
            pieces[number, index].append(copy)

    barrier = pltpu.get_barrier_semaphore()

    def hail(device):
        pl.semaphore_signal(barrier, inc=1, device_id=device, device_id_type=MESH)

    for step in range(1, group):
        hail({"ulysses": base + (member + step) % group})
    hail(across)

    @pl.when(has_far)
    def _():
        hail(far)
        hail(behind)

    @pl.when(has_onward)
    def _():
        hail(onward)

    lists = [
        pltpu.make_async_copy(tiles_in, tiles, list_sem.at[0]),
        pltpu.make_async_copy(counts_in, counts, list_sem.at[1]),
    ]
    for copy in lists:
        copy.start()
    for index, span in enumerate(key_cuts):
        for number in (0, 1):
            take(number, index, span)

    for copy in lists:
        copy.wait()
    across_frame, far_frame = frame - turn, frame + turn
    picks = [
        nth_tiles(listing(tiles, counts, reader, frame, frame_tiles, frames), frame_tiles, count)
        for reader in (across_frame, far_frame)
    ]
    pl.semaphore_wait(
        barrier, group + jnp.where(has_far, 2, 0) + jnp.where(has_onward, 1, 0)
    )
    for index, span in enumerate(key_cuts):
        for number in (0, 1):
            trade(number, index, span)

    def lot(ref, chunk):
        return ref if spans[chunk][1] == widest else ref.at[:, :, pl.ds(0, spans[chunk][1])]

    def edge_copy(phase, way, chunk, device):
        return remote(
            lot(outgoing.at[phase, way, chunk], chunk), lot(incoming.at[phase, way, chunk], chunk),
            edge_send.at[phase, way, chunk], edge_recv.at[phase, way, chunk], device,
        )

    def relay_in(phase, chunk):
        return remote(
            lot(outgoing.at[phase, 1, chunk], chunk), lot(relay.at[phase, chunk], chunk),
            edge_send.at[phase, 1, chunk], relay_recv.at[phase, chunk], across,
        )

    def relay_out(phase, chunk):
        return remote(
            lot(relay.at[phase, chunk], chunk), lot(incoming.at[phase, 1, chunk], chunk),
            relay_send.at[phase, chunk], edge_recv.at[phase, 1, chunk], onward,
        )

    def passes(phase, chunk):
        return has_onward & relayed(phase, chunk, other_share, slabs, spans)

    def send_across(phase, chunk):
        edge_copy(phase, 0, chunk, across).start()

    def send_far(phase, chunk):
        around = relayed(phase, chunk, my_share, slabs, spans)

        @pl.when(has_far & jnp.logical_not(around))
        def _():
            edge_copy(phase, 1, chunk, far).start()

        @pl.when(has_far & around)
        def _():
            relay_in(phase, chunk).start()

    def pass_on(phase, chunk):
        @pl.when(passes(phase, chunk))
        def _():
            relay_in(phase, chunk).wait_recv()
            relay_out(phase, chunk).start()

    def receive_edges(phase, chunk):
        edge_copy(phase, 0, chunk, across).wait_recv()

        @pl.when(has_far)
        def _():
            edge_copy(phase, 1, chunk, far).wait_recv()

    def settle_edges(phase, chunk):
        edge_copy(phase, 0, chunk, across).wait_send()

        @pl.when(has_far)
        def _():
            edge_copy(phase, 1, chunk, far).wait_send()

        @pl.when(passes(phase, chunk))
        def _():
            relay_out(phase, chunk).wait_send()

    for index, span in enumerate(key_cuts):
        for number in (0, 1):
            for copy in pieces[number, index]:
                copy.wait()
        for chunk in range(*span):
            columns = pl.ds(*spans[chunk])
            size = spans[chunk][1]
            for number in (0, 1):
                for way in range(2):
                    for spot in range(count):
                        chosen = own[number, pl.ds(0, TILE), columns]
                        for tile in range(1, frame_tiles):
                            here = own[number, pl.ds(tile * TILE, TILE), columns]
                            chosen = jnp.where(picks[way][spot][tile], here, chosen)
                        outgoing[0, way, chunk, number, pl.ds(spot * TILE, TILE), pl.ds(0, size)] = chosen
            send_far(0, chunk)
            send_across(0, chunk)
        if index == 0:
            for piece, part in enumerate(query_cuts):
                for number in (2, 3):
                    take(number, piece, part)
                    trade(number, piece, part)

    @pl.when(jnp.logical_not(has_far))
    def _():
        for phase in range(2):
            for chunk in range(chunks):
                incoming[phase, 1, chunk] = jnp.zeros((2, edge, widest), BF16)

    blocks, step_rows = bias.shape[0], bias.shape[2]
    across_rows = listing(tiles, counts, frame, across_frame, frame_tiles, frames)
    own_masks = listing(tiles, counts, frame, frame, frame_tiles, frames)
    far_rows = listing(tiles, counts, frame, far_frame, frame_tiles, frames)

    def edge_hits(masks):
        picked = nth_tiles(masks, frame_tiles, count)
        hits = []
        for spot in range(count):
            bit = jnp.int32(0)
            for tile in range(frame_tiles):
                bit = bit + jnp.where(picked[spot][tile], 1 << tile, 0)
            hits.append([(mask & bit) != 0 for mask in masks])
        return hits

    hits = edge_hits(across_rows)
    hits += [[((mask >> tile) & 1) == 1 for mask in own_masks] for tile in range(frame_tiles)]
    hits += edge_hits(far_rows)
    block_tiles = step_rows // TILE
    inner = lax.broadcasted_iota(jnp.int32, (1, step_rows), 1) // TILE
    for number, row in enumerate(hits):
        for block in range(blocks):
            line = jnp.full((1, step_rows), DEAD, F32)
            for spot in range(block_tiles):
                level = jnp.where(row[block * block_tiles + spot], 0.0, DEAD)
                line = jnp.where(inner == spot, level, line)
            bias[block, pl.ds(number, 1)] = line

    leaving = {}

    def share(phase, chunk):
        start, size = spans[chunk]
        target, columns = (early, late)[phase], pl.ds(start, size)
        there = lanes_of(member, start, size)
        copies = [pltpu.make_async_copy(
            result.at[phase, :, rows_of(member), columns], target.at[:, :, there],
            out_near.at[phase, chunk],
        )]
        for step in range(1, group):
            peer = (member + step) % group
            copies.append(remote(
                result.at[phase, :, rows_of(peer), columns], target.at[:, :, there],
                out_send.at[phase, chunk, step - 1], out_recv.at[phase, chunk, step - 1],
                {"ulysses": base + peer},
            ))
        for copy in copies:
            copy.start()
        leaving[phase, chunk] = copies

    def attend(chunk):
        @pl.loop(0, spans[chunk][1] // LANES)
        def _(pair):
            inside = pl.ds(pl.multiple_of(pair * LANES, LANES), LANES)
            lanes = pl.ds(pl.multiple_of(spans[chunk][0] + pair * LANES, LANES), LANES)

            def stacked(number):
                return jnp.concatenate([
                    incoming[0, 0, chunk, number, :, inside], own[number, :, lanes],
                    incoming[0, 1, chunk, number, :, inside],
                ])

            for block in range(blocks):
                span = pl.ds(block * step_rows, step_rows)
                out, grad_rows, key_part, value_part = heads_math(
                    own[2, span, lanes], own[3, span, lanes], stacked(0), stacked(1), bias[block],
                )
                result[0, 0, span, lanes] = out
                result[0, 1, span, lanes] = grad_rows
                for number, part in enumerate((key_part, value_part)):
                    if block:
                        part = part + sums[number]
                    if block + 1 < blocks:
                        sums[number] = part
                        continue
                    outgoing[1, 0, chunk, number, :, inside] = part[:edge].astype(BF16)
                    parts[number, :, lanes] = part[edge : edge + frame_rows]
                    outgoing[1, 1, chunk, number, :, inside] = part[edge + frame_rows :].astype(BF16)

    for chunk in range(chunks + LAG):
        if chunk < chunks:
            pass_on(0, chunk)
        ready = chunk - LAG
        if ready < 0:
            continue
        for piece, part in enumerate(query_cuts):
            if part[0] == ready:
                for number in (2, 3):
                    for copy in pieces[number, piece]:
                        copy.wait()
        receive_edges(0, ready)
        attend(ready)
        send_far(1, ready)
        if ready >= HOLD:
            send_across(1, ready - HOLD)
        share(0, ready)

    for chunk in range(max(0, chunks - HOLD), chunks):
        send_across(1, chunk)
    for chunk in range(chunks):
        settle_edges(0, chunk)

    def gather(chunk):
        columns, size = pl.ds(*spans[chunk]), spans[chunk][1]
        for number in range(2):
            for tile in range(frame_tiles):
                span = pl.ds(tile * TILE, TILE)
                total = parts[number, span, columns]
                for way in range(2):
                    for spot in range(count):
                        part = incoming[1, way, chunk, number, pl.ds(spot * TILE, TILE), pl.ds(0, size)]
                        total = total + jnp.where(picks[way][spot][tile], part.astype(F32), 0.0)
                result[1, number, span, columns] = total.astype(BF16)
        share(1, chunk)

    for chunk in range(chunks + LAG):
        if chunk < chunks:
            pass_on(1, chunk)
        ready = chunk - LAG
        if ready < 0:
            continue
        for copy in leaving.pop((0, ready)):
            copy.wait()
        receive_edges(1, ready)
        gather(ready)

    for chunk in range(chunks):
        settle_edges(1, chunk)
        for copy in leaving.pop((1, chunk)):
            copy.wait()


def flush_kernel(early, late, *refs):
    sems = refs[4]
    copies = [
        pltpu.make_async_copy((early, late)[n // 2].at[n % 2], refs[n], sems.at[n])
        for n in range(4)
    ]
    for copy in copies:
        copy.start()
    for copy in copies:
        copy.wait()


def per_device(slabs, group, queries, key_vectors, value_vectors, grad_out, key_tiles, tile_counts):
    rows, columns = queries.shape
    width = columns // group
    frame_rows = rows * group
    frame_tiles = frame_rows // TILE
    count = max(1, frame_tiles // 8)
    edge = count * TILE
    ext_rows = frame_rows + 2 * edge
    spans = chunk_spans(width)
    chunks, chunk_width = len(spans), max(size for _, size in spans)
    step_rows = block_rows(frame_rows, ext_rows)
    blocks = frame_rows // step_rows
    key_pieces, query_pieces = len(cuts(chunks, 1)), len(cuts(chunks, max(1, chunks // 2)))
    most = max(key_pieces, query_pieces)

    vmem = pl.BlockSpec(memory_space=pltpu.VMEM)
    hbm = pl.BlockSpec(memory_space=pltpu.HBM)
    dma = pltpu.SemaphoreType.DMA
    arguments = [
        pltpu.with_memory_space_constraint(value, pltpu.HBM)
        for value in (key_tiles.T, tile_counts, queries, key_vectors, value_vectors, grad_out)
    ]
    results = pl.pallas_call(
        functools.partial(fused_kernel, group, slabs, count, spans),
        out_shape=(jax.ShapeDtypeStruct((2, rows, columns), BF16),) * 2,
        in_specs=[hbm] * 6,
        out_specs=(vmem,) * 2,
        scratch_shapes=[
            pltpu.VMEM((4, frame_rows, width), BF16),
            pltpu.VMEM((blocks, ext_rows // TILE, step_rows), F32),
            pltpu.VMEM((2, 2, chunks, 2, edge, chunk_width), BF16),
            pltpu.VMEM((2, 2, chunks, 2, edge, chunk_width), BF16),
            pltpu.VMEM((2, chunks, 2, edge, chunk_width), BF16),
            pltpu.VMEM((2, frame_rows, width), F32),
            pltpu.VMEM((2, ext_rows if blocks > 1 else TILE, LANES), F32),
            pltpu.VMEM((2, 2, frame_rows, width), BF16),
            dma((4, most, group - 1)), dma((4, most, group - 1)), dma((4, most)),
            dma((2, 2, chunks)), dma((2, 2, chunks)), dma((2, chunks)), dma((2, chunks)),
            dma((2, chunks, group - 1)), dma((2, chunks, group - 1)), dma((2, chunks)),
            pltpu.SMEM(key_tiles.T.shape, jnp.int32), pltpu.SMEM(tile_counts.shape, jnp.int32), dma((2,)),
        ],
        compiler_params=pltpu.CompilerParams(
            collective_id=0, has_side_effects=True, vmem_limit_bytes=32 << 20
        ),
        name="frame_attention",
    )(*arguments)
    return pl.pallas_call(
        flush_kernel,
        out_shape=(jax.ShapeDtypeStruct((rows, columns), BF16),) * 4,
        in_specs=[vmem] * 2,
        out_specs=(hbm,) * 4,
        scratch_shapes=[dma((4,))],
        compiler_params=pltpu.CompilerParams(vmem_limit_bytes=16 << 20),
        name="flush_results",
    )(*results)


def solution(mesh):
    tokens = P(("clips", "tm", "ulysses"), None)
    group = mesh.shape["ulysses"] // FRAMES_SLAB
    return jax.shard_map(
        functools.partial(per_device, mesh.shape["tm"], group),
        mesh=mesh,
        in_specs=(tokens, tokens, tokens, tokens, P("clips", None), P("clips")),
        out_specs=(tokens,) * 4,
        check_vma=False,
    )
```

```python
import functools

import jax
import jax.numpy as jnp
from jax import lax
from jax.experimental import pallas as pl
from jax.experimental.pallas import tpu as pltpu
from jax.sharding import PartitionSpec as P

HEAD_DIM = 64
TILE = 64
FRAMES_SLAB = 2
LANES = 128
DEAD = -1e30
BLOCK_LIMIT = 384 * 512
CHUNK = 256
LAG = 1
HOLD = 1
MESH = pl.DeviceIdType.MESH
BF16 = jnp.bfloat16
F32 = jnp.float32


def remote(source, target, send, receive, device):
    return pltpu.make_async_remote_copy(
        src_ref=source, dst_ref=target, send_sem=send, recv_sem=receive,
        device_id=device, device_id_type=MESH,
    )


def heads_math(query, grad, keys, values, bias):
    scale = HEAD_DIM ** (-0.5)
    lanes = lax.broadcasted_iota(jnp.int32, query.shape, 1)
    first = lanes < HEAD_DIM
    nothing = jnp.zeros_like(query)
    query = query * jnp.asarray(scale, BF16)
    queries = jnp.concatenate([jnp.where(first, query, nothing), jnp.where(first, nothing, query)])
    grads = jnp.concatenate([jnp.where(first, grad, nothing), jnp.where(first, nothing, grad)])
    rows, columns = keys.shape[0], queries.shape[0]

    def dot(left, right, dims):
        return lax.dot_general(left, right, (dims, ((), ())), preferred_element_type=F32)

    def pick(both):
        return jnp.where(first, both[: columns // 2], both[columns // 2 :])

    scores = dot(keys, queries, ((1,), (1,)))
    bias = jnp.concatenate([bias, bias], axis=1)
    scores = scores.reshape(rows // TILE, TILE, columns) + bias[:, None, :]
    scores = scores.reshape(rows, columns)
    expo = jnp.exp(scores - jnp.max(scores, axis=0, keepdims=True))
    probs = expo * (1.0 / jnp.sum(expo, axis=0, keepdims=True))
    probs_low = probs.astype(BF16)
    grad_probs = dot(values, grads, ((1,), (1,)))
    delta = jnp.sum(probs * grad_probs, axis=0, keepdims=True)
    grad_low = (probs * (grad_probs - delta)).astype(BF16)
    attended = pick(dot(probs_low, values, ((0,), (0,)))).astype(BF16)
    grad_query = (pick(dot(grad_low, keys, ((0,), (0,)))) * scale).astype(BF16)
    key_part = dot(grad_low, queries, ((1,), (0,)))
    value_part = dot(probs_low, grads, ((1,), (0,)))
    return attended, grad_query, key_part, value_part


def block_rows(frame_rows, ext_rows):
    tiles = frame_rows // TILE
    for step in range(tiles, 0, -1):
        if tiles % step == 0 and 2 * step * TILE * ext_rows <= BLOCK_LIMIT:
            return step * TILE
    return TILE


def listing(tiles, counts, reader, source, frame_tiles, frames):
    reader = jnp.clip(reader, 0, frames - 1)
    masks = []
    for row in range(frame_tiles):
        tile = reader * frame_tiles + row
        mask = jnp.int32(0)
        for slot in range(tiles.shape[0]):
            inside = tiles[slot, tile] - source * frame_tiles
            good = (inside >= 0) & (inside < frame_tiles) & (slot < counts[tile])
            bit = lax.shift_left(jnp.int32(1), jnp.clip(inside, 0, frame_tiles - 1))
            mask = mask | jnp.where(good, bit, 0)
        masks.append(mask)
    return masks


def nth_tiles(masks, frame_tiles, count):
    union = functools.reduce(lambda left, right: left | right, masks)
    seen = jnp.int32(0)
    picked = [[] for _ in range(count)]
    for tile in range(frame_tiles):
        bit = (union >> tile) & 1
        for spot in range(count):
            picked[spot].append((bit == 1) & (seen == spot))
        seen = seen + bit
    return picked


def chunk_spans(width):
    sizes = [LANES] * (width // LANES)
    if width % CHUNK == 0 and width > CHUNK:
        sizes = [LANES] + [CHUNK] * (width // CHUNK - 1) + [CHUNK - LANES]
    return [(sum(sizes[:n]), size) for n, size in enumerate(sizes)]


def relayed(phase, chunk, share, slabs, spans):
    if phase == 0 and chunk + 1 == len(spans):
        return share < 0
    if phase == 0:
        return ((chunk + 1) * share) // slabs > (chunk * share) // slabs
    start, size = spans[chunk]
    total = spans[-1][0] + spans[-1][1]
    return (start + size) * slabs <= total * share


def cuts(chunks, first):
    spans, start, size = [], 0, first
    while start < chunks:
        stop = min(chunks, start + size)
        spans.append((start, stop))
        start, size = stop, size + 1
    return spans


def fused_kernel(
    group, slabs, count, spans, tiles_in, counts_in, q_in, k_in, v_in, g_in,
    early, late,
    own, bias, outgoing, incoming, relay, parts, sums, result,
    send, recv, near, edge_send, edge_recv, relay_send, relay_recv,
    out_send, out_recv, out_near, tiles, counts, list_sem, lead, lead_sem, offer, offered,
    offer_send, offer_recv,
):
    place, slab = lax.axis_index("ulysses"), lax.axis_index("tm")
    side, member = place // group, place % group
    base = side * group
    frames = slabs * FRAMES_SLAB
    frame = slab * FRAMES_SLAB + side
    rows, frame_rows, width = q_in.shape[0], own.shape[1], own.shape[2]
    chunks, widest = len(spans), outgoing.shape[5]
    edge = count * TILE
    frame_tiles = frame_rows // TILE

    turn = 2 * side - 1
    far_slab, onward_slab = slab + turn, slab - turn
    has_far = (far_slab >= 0) & (far_slab < slabs)
    has_onward = (onward_slab >= 0) & (onward_slab < slabs)
    across = {"ulysses": (1 - side) * group + member}
    far = {**across, "tm": jnp.clip(far_slab, 0, slabs - 1)}
    onward = {"tm": jnp.clip(onward_slab, 0, slabs - 1)}
    behind = {"tm": jnp.clip(far_slab, 0, slabs - 1)}
    from_end, from_start = slabs - 1 - slab, slab
    my_share = jnp.where(side == 1, from_end, from_start)
    other_share = jnp.where(side == 1, from_start, from_end)

    def lanes_of(which, start, size):
        return pl.ds(pl.multiple_of(which * width + start, LANES), size)

    def rows_of(which):
        return pl.ds(pl.multiple_of(which * rows, TILE), rows)

    sources = (k_in, v_in, q_in, g_in)
    pieces, nearby, sent = {}, {}, []

    def arrive(number, index):
        for copy in nearby.pop((number, index), []):
            copy.wait()
        for copy in pieces[number, index]:
            copy.wait_recv()

    key_cuts, query_cuts = cuts(chunks, 1), cuts(chunks, max(1, chunks // 2))

    def take(number, index, span):
        start = spans[span[0]][0]
        size = sum(spans[span[1] - 1]) - start
        copy = pltpu.make_async_copy(
            sources[number].at[:, lanes_of(member, start, size)],
            own.at[number, rows_of(member), pl.ds(start, size)], near.at[number, index],
        )
        copy.start()
        nearby[number, index], pieces[number, index] = [copy], []

    def trade(number, index, span):
        start = spans[span[0]][0]
        size = sum(spans[span[1] - 1]) - start
        for step in range(1, group):
            peer = (member + step) % group
            source = sources[number].at[:, lanes_of(peer, start, size)]
            if number < 2 and index == 0:
                source = lead.at[number, step - 1]
            copy = remote(
                source, own.at[number, rows_of(member), pl.ds(start, size)],
                send.at[number, index, step - 1], recv.at[number, index, step - 1],
                {"ulysses": base + peer},
            )
            copy.start()
            pieces[number, index].append(copy)
            sent.append(copy)

    barrier = pltpu.get_barrier_semaphore()
    eager, own_tiles = group == FRAMES_SLAB, rows // TILE

    def opposite(step):
        return {"ulysses": (1 - side) * group + (member + step) % group}

    def hail(device):
        pl.semaphore_signal(barrier, inc=1, device_id=device, device_id_type=MESH)

    for step in range(1, group):
        hail({"ulysses": base + (member + step) % group})
    for step in range(group if eager else 1):
        hail(opposite(step))

    @pl.when(has_far)
    def _():
        hail(far)
        hail(behind)

    @pl.when(has_onward)
    def _():
        hail(onward)

    lists = [
        pltpu.make_async_copy(tiles_in, tiles, list_sem.at[0]),
        pltpu.make_async_copy(counts_in, counts, list_sem.at[1]),
    ]
    for copy in lists:
        copy.start()
    leads = []
    for number in (0, 1):
        for step in range(1, group):
            peer = (member + step) % group
            copy = pltpu.make_async_copy(
                sources[number].at[:, lanes_of(peer, 0, spans[0][1])],
                lead.at[number, step - 1], lead_sem.at[number, step - 1],
            )
            copy.start()
            leads.append(copy)
    for index, span in enumerate(key_cuts):
        for number in (0, 1):
            take(number, index, span)

    for copy in lists:
        copy.wait()
    across_frame, far_frame = frame - turn, frame + turn
    picks = [
        nth_tiles(listing(tiles, counts, reader, frame, frame_tiles, frames), frame_tiles, count)
        for reader in (across_frame, far_frame)
    ]
    def offer_copy(step):
        return remote(
            offer.at[step], offered.at[step], offer_send.at[step], offer_recv.at[step],
            opposite(step),
        )

    def any_of(flags):
        return functools.reduce(lambda left, right: left | right, flags)

    def candidate(step, number, inner):
        start = inner * TILE
        if step:
            return lead[number, step - 1, pl.ds(start, TILE)]
        place_rows = pl.ds(pl.multiple_of(member * rows + start, TILE), TILE)
        return own[number, place_rows, pl.ds(0, spans[0][1])]

    for copy in leads:
        copy.wait()
    if eager:
        for number in (0, 1):
            for copy in nearby.pop((number, 0)):
                copy.wait()
            for step in range(group):
                for spot in range(count):
                    chosen = candidate(step, number, 0)
                    for inner in range(1, own_tiles):
                        flag = any_of([
                            (member == m) & picks[0][spot][m * own_tiles + inner]
                            for m in range(group)
                        ])
                        chosen = jnp.where(flag, candidate(step, number, inner), chosen)
                    offer[step, number, pl.ds(spot * TILE, TILE)] = chosen
    pl.semaphore_wait(
        barrier, (2 * group - 1 if eager else group) + jnp.where(has_far, 2, 0) + jnp.where(has_onward, 1, 0)
    )
    for index, span in enumerate(key_cuts):
        for number in (0, 1):
            trade(number, index, span)
        if eager and index == 0:
            for step in range(group):
                offer_copy(step).start()

    def lot(ref, chunk):
        return ref if spans[chunk][1] == widest else ref.at[:, :, pl.ds(0, spans[chunk][1])]

    def edge_copy(phase, way, chunk, device):
        return remote(
            lot(outgoing.at[phase, way, chunk], chunk), lot(incoming.at[phase, way, chunk], chunk),
            edge_send.at[phase, way, chunk], edge_recv.at[phase, way, chunk], device,
        )

    def relay_in(phase, chunk):
        return remote(
            lot(outgoing.at[phase, 1, chunk], chunk), lot(relay.at[phase, chunk], chunk),
            edge_send.at[phase, 1, chunk], relay_recv.at[phase, chunk], across,
        )

    def relay_out(phase, chunk):
        return remote(
            lot(relay.at[phase, chunk], chunk), lot(incoming.at[phase, 1, chunk], chunk),
            relay_send.at[phase, chunk], edge_recv.at[phase, 1, chunk], onward,
        )

    def passes(phase, chunk):
        return has_onward & relayed(phase, chunk, other_share, slabs, spans)

    def send_across(phase, chunk):
        if eager and (phase, chunk) == (0, 0):
            return
        edge_copy(phase, 0, chunk, across).start()

    def send_far(phase, chunk):
        around = relayed(phase, chunk, my_share, slabs, spans)

        @pl.when(has_far & jnp.logical_not(around))
        def _():
            edge_copy(phase, 1, chunk, far).start()

        @pl.when(has_far & around)
        def _():
            relay_in(phase, chunk).start()

    def pass_on(phase, chunk):
        @pl.when(passes(phase, chunk))
        def _():
            relay_in(phase, chunk).wait_recv()
            relay_out(phase, chunk).start()

    def accept():
        size = spans[0][1]
        for step in range(group):
            offer_copy(step).wait_recv()
        for spot in range(count):
            rows_here = pl.ds(spot * TILE, TILE)
            for number in (0, 1):
                chosen = offered[0, number, rows_here]
                for step in range(1, group):
                    flag = any_of([
                        ((member - step + group) % group == tile // own_tiles) & across_picks[spot][tile]
                        for tile in range(frame_tiles)
                    ])
                    chosen = jnp.where(flag, offered[step, number, rows_here], chosen)
                incoming[0, 0, 0, number, rows_here, pl.ds(0, size)] = chosen

    def receive_edges(phase, chunk):
        if eager and (phase, chunk) == (0, 0):
            accept()
        else:
            edge_copy(phase, 0, chunk, across).wait_recv()

        @pl.when(has_far)
        def _():
            edge_copy(phase, 1, chunk, far).wait_recv()

    def settle_edges(phase, chunk):
        if eager and (phase, chunk) == (0, 0):
            for step in range(group):
                offer_copy(step).wait_send()
        else:
            edge_copy(phase, 0, chunk, across).wait_send()

        @pl.when(has_far)
        def _():
            edge_copy(phase, 1, chunk, far).wait_send()

        @pl.when(passes(phase, chunk))
        def _():
            relay_out(phase, chunk).wait_send()

    for index, span in enumerate(key_cuts):
        for number in (0, 1):
            arrive(number, index)
        for chunk in range(*span):
            columns = pl.ds(*spans[chunk])
            size = spans[chunk][1]
            for number in (0, 1):
                for way in range(2):
                    for spot in range(count):
                        chosen = own[number, pl.ds(0, TILE), columns]
                        for tile in range(1, frame_tiles):
                            here = own[number, pl.ds(tile * TILE, TILE), columns]
                            chosen = jnp.where(picks[way][spot][tile], here, chosen)
                        outgoing[0, way, chunk, number, pl.ds(spot * TILE, TILE), pl.ds(0, size)] = chosen
            send_far(0, chunk)
            send_across(0, chunk)
        if index == 0:
            for piece, part in enumerate(query_cuts):
                for number in (2, 3):
                    take(number, piece, part)
                    trade(number, piece, part)

    @pl.when(jnp.logical_not(has_far))
    def _():
        for phase in range(2):
            for chunk in range(chunks):
                incoming[phase, 1, chunk] = jnp.zeros((2, edge, widest), BF16)

    blocks, step_rows = bias.shape[0], bias.shape[2]
    across_rows = listing(tiles, counts, frame, across_frame, frame_tiles, frames)
    across_picks = nth_tiles(across_rows, frame_tiles, count)
    own_masks = listing(tiles, counts, frame, frame, frame_tiles, frames)
    far_rows = listing(tiles, counts, frame, far_frame, frame_tiles, frames)

    def edge_hits(masks):
        picked = nth_tiles(masks, frame_tiles, count)
        hits = []
        for spot in range(count):
            bit = jnp.int32(0)
            for tile in range(frame_tiles):
                bit = bit + jnp.where(picked[spot][tile], 1 << tile, 0)
            hits.append([(mask & bit) != 0 for mask in masks])
        return hits

    hits = edge_hits(across_rows)
    hits += [[((mask >> tile) & 1) == 1 for mask in own_masks] for tile in range(frame_tiles)]
    hits += edge_hits(far_rows)
    block_tiles = step_rows // TILE
    inner = lax.broadcasted_iota(jnp.int32, (1, step_rows), 1) // TILE
    for number, row in enumerate(hits):
        for block in range(blocks):
            line = jnp.full((1, step_rows), DEAD, F32)
            for spot in range(block_tiles):
                level = jnp.where(row[block * block_tiles + spot], 0.0, DEAD)
                line = jnp.where(inner == spot, level, line)
            bias[block, pl.ds(number, 1)] = line

    leaving = {}

    def share(phase, chunk):
        start, size = spans[chunk]
        target, columns = (early, late)[phase], pl.ds(start, size)
        there = lanes_of(member, start, size)
        copies = [pltpu.make_async_copy(
            result.at[phase, :, rows_of(member), columns], target.at[:, :, there],
            out_near.at[phase, chunk],
        )]
        for step in range(1, group):
            peer = (member + step) % group
            copies.append(remote(
                result.at[phase, :, rows_of(peer), columns], target.at[:, :, there],
                out_send.at[phase, chunk, step - 1], out_recv.at[phase, chunk, step - 1],
                {"ulysses": base + peer},
            ))
        for copy in copies:
            copy.start()
        leaving[phase, chunk] = copies

    def attend(chunk):
        @pl.loop(0, spans[chunk][1] // LANES)
        def _(pair):
            inside = pl.ds(pl.multiple_of(pair * LANES, LANES), LANES)
            lanes = pl.ds(pl.multiple_of(spans[chunk][0] + pair * LANES, LANES), LANES)

            def stacked(number):
                return jnp.concatenate([
                    incoming[0, 0, chunk, number, :, inside], own[number, :, lanes],
                    incoming[0, 1, chunk, number, :, inside],
                ])

            for block in range(blocks):
                span = pl.ds(block * step_rows, step_rows)
                out, grad_rows, key_part, value_part = heads_math(
                    own[2, span, lanes], own[3, span, lanes], stacked(0), stacked(1), bias[block],
                )
                result[0, 0, span, lanes] = out
                result[0, 1, span, lanes] = grad_rows
                for number, part in enumerate((key_part, value_part)):
                    if block:
                        part = part + sums[number]
                    if block + 1 < blocks:
                        sums[number] = part
                        continue
                    outgoing[1, 0, chunk, number, :, inside] = part[:edge].astype(BF16)
                    parts[number, :, lanes] = part[edge : edge + frame_rows]
                    outgoing[1, 1, chunk, number, :, inside] = part[edge + frame_rows :].astype(BF16)

    for chunk in range(chunks + LAG):
        if chunk < chunks:
            pass_on(0, chunk)
        ready = chunk - LAG
        if ready < 0:
            continue
        for piece, part in enumerate(query_cuts):
            if part[0] == ready:
                for number in (2, 3):
                    arrive(number, piece)
        receive_edges(0, ready)
        attend(ready)
        send_far(1, ready)
        if ready >= HOLD:
            send_across(1, ready - HOLD)
        share(0, ready)

    for chunk in range(max(0, chunks - HOLD), chunks):
        send_across(1, chunk)
    for copy in sent:
        copy.wait_send()
    for chunk in range(chunks):
        settle_edges(0, chunk)

    def gather(chunk):
        columns, size = pl.ds(*spans[chunk]), spans[chunk][1]
        for number in range(2):
            for tile in range(frame_tiles):
                span = pl.ds(tile * TILE, TILE)
                total = parts[number, span, columns]
                for way in range(2):
                    for spot in range(count):
                        part = incoming[1, way, chunk, number, pl.ds(spot * TILE, TILE), pl.ds(0, size)]
                        total = total + jnp.where(picks[way][spot][tile], part.astype(F32), 0.0)
                result[1, number, span, columns] = total.astype(BF16)
        share(1, chunk)

    for chunk in range(chunks + LAG):
        if chunk < chunks:
            pass_on(1, chunk)
        ready = chunk - LAG
        if ready < 0:
            continue
        for copy in leaving.pop((0, ready)):
            copy.wait()
        if ready:
            settle_edges(1, ready - 1)
        if ready > 1:
            for copy in leaving.pop((1, ready - 2)):
                copy.wait()
        receive_edges(1, ready)
        gather(ready)

    settle_edges(1, chunks - 1)
    for copies in leaving.values():
        for copy in copies:
            copy.wait()


def flush_kernel(early, late, *refs):
    sems = refs[4]
    copies = [
        pltpu.make_async_copy((early, late)[n // 2].at[n % 2], refs[n], sems.at[n])
        for n in range(4)
    ]
    for copy in copies:
        copy.start()
    for copy in copies:
        copy.wait()


def per_device(slabs, group, queries, key_vectors, value_vectors, grad_out, key_tiles, tile_counts):
    rows, columns = queries.shape
    width = columns // group
    frame_rows = rows * group
    frame_tiles = frame_rows // TILE
    count = max(1, frame_tiles // 8)
    edge = count * TILE
    ext_rows = frame_rows + 2 * edge
    spans = chunk_spans(width)
    chunks, chunk_width = len(spans), max(size for _, size in spans)
    step_rows = block_rows(frame_rows, ext_rows)
    blocks = frame_rows // step_rows
    key_pieces, query_pieces = len(cuts(chunks, 1)), len(cuts(chunks, max(1, chunks // 2)))
    most = max(key_pieces, query_pieces)

    vmem = pl.BlockSpec(memory_space=pltpu.VMEM)
    hbm = pl.BlockSpec(memory_space=pltpu.HBM)
    dma = pltpu.SemaphoreType.DMA
    arguments = [
        pltpu.with_memory_space_constraint(value, pltpu.HBM)
        for value in (key_tiles.T, tile_counts, queries, key_vectors, value_vectors, grad_out)
    ]
    results = pl.pallas_call(
        functools.partial(fused_kernel, group, slabs, count, spans),
        out_shape=(jax.ShapeDtypeStruct((2, rows, columns), BF16),) * 2,
        in_specs=[hbm] * 6,
        out_specs=(vmem,) * 2,
        scratch_shapes=[
            pltpu.VMEM((4, frame_rows, width), BF16),
            pltpu.VMEM((blocks, ext_rows // TILE, step_rows), F32),
            pltpu.VMEM((2, 2, chunks, 2, edge, chunk_width), BF16),
            pltpu.VMEM((2, 2, chunks, 2, edge, chunk_width), BF16),
            pltpu.VMEM((2, chunks, 2, edge, chunk_width), BF16),
            pltpu.VMEM((2, frame_rows, width), F32),
            pltpu.VMEM((2, ext_rows if blocks > 1 else TILE, LANES), F32),
            pltpu.VMEM((2, 2, frame_rows, width), BF16),
            dma((4, most, group - 1)), dma((4, most, group - 1)), dma((4, most)),
            dma((2, 2, chunks)), dma((2, 2, chunks)), dma((2, chunks)), dma((2, chunks)),
            dma((2, chunks, group - 1)), dma((2, chunks, group - 1)), dma((2, chunks)),
            pltpu.SMEM(key_tiles.T.shape, jnp.int32), pltpu.SMEM(tile_counts.shape, jnp.int32), dma((2,)),
            pltpu.VMEM((2, group - 1, rows, spans[0][1]), BF16), dma((2, group - 1)),
            pltpu.VMEM((group, 2, edge, spans[0][1]), BF16), pltpu.VMEM((group, 2, edge, spans[0][1]), BF16),
            dma((group,)), dma((group,)),
        ],
        compiler_params=pltpu.CompilerParams(
            collective_id=0, has_side_effects=True, vmem_limit_bytes=32 << 20
        ),
        name="frame_attention",
    )(*arguments)
    return pl.pallas_call(
        flush_kernel,
        out_shape=(jax.ShapeDtypeStruct((rows, columns), BF16),) * 4,
        in_specs=[vmem] * 2,
        out_specs=(hbm,) * 4,
        scratch_shapes=[dma((4,))],
        compiler_params=pltpu.CompilerParams(vmem_limit_bytes=16 << 20),
        name="flush_results",
    )(*results)


def solution(mesh):
    tokens = P(("clips", "tm", "ulysses"), None)
    group = mesh.shape["ulysses"] // FRAMES_SLAB
    return jax.shard_map(
        functools.partial(per_device, mesh.shape["tm"], group),
        mesh=mesh,
        in_specs=(tokens, tokens, tokens, tokens, P("clips", None), P("clips")),
        out_specs=(tokens,) * 4,
        check_vma=False,
    )
```

```python
import functools

import jax
import jax.numpy as jnp
from jax import lax
from jax.experimental import pallas as pl
from jax.experimental.pallas import tpu as pltpu
from jax.sharding import PartitionSpec as P

HEAD_DIM = 64
TILE = 64
FRAMES_SLAB = 2
LANES = 128
DEAD = -1e30
BLOCK_LIMIT = 384 * 512
CHUNK = 256
LAG = 1
HOLD = 1
MESH = pl.DeviceIdType.MESH
BF16 = jnp.bfloat16
F32 = jnp.float32


def remote(source, target, send, receive, device):
    return pltpu.make_async_remote_copy(
        src_ref=source, dst_ref=target, send_sem=send, recv_sem=receive,
        device_id=device, device_id_type=MESH,
    )


def heads_math(query, grad, keys, values, bias):
    scale = HEAD_DIM ** (-0.5)
    lanes = lax.broadcasted_iota(jnp.int32, query.shape, 1)
    first = lanes < HEAD_DIM
    nothing = jnp.zeros_like(query)
    query = query * jnp.asarray(scale, BF16)
    queries = jnp.concatenate([jnp.where(first, query, nothing), jnp.where(first, nothing, query)])
    grads = jnp.concatenate([jnp.where(first, grad, nothing), jnp.where(first, nothing, grad)])
    rows, columns = keys.shape[0], queries.shape[0]

    def dot(left, right, dims):
        return lax.dot_general(left, right, (dims, ((), ())), preferred_element_type=F32)

    def pick(both):
        return jnp.where(first, both[: columns // 2], both[columns // 2 :])

    scores = dot(keys, queries, ((1,), (1,)))
    bias = jnp.concatenate([bias, bias], axis=1)
    scores = scores.reshape(rows // TILE, TILE, columns) + bias[:, None, :]
    scores = scores.reshape(rows, columns)
    expo = jnp.exp(scores - jnp.max(scores, axis=0, keepdims=True))
    probs = expo * (1.0 / jnp.sum(expo, axis=0, keepdims=True))
    probs_low = probs.astype(BF16)
    grad_probs = dot(values, grads, ((1,), (1,)))
    delta = jnp.sum(probs * grad_probs, axis=0, keepdims=True)
    grad_low = (probs * (grad_probs - delta)).astype(BF16)
    attended = pick(dot(probs_low, values, ((0,), (0,)))).astype(BF16)
    grad_query = (pick(dot(grad_low, keys, ((0,), (0,)))) * scale).astype(BF16)
    key_part = dot(grad_low, queries, ((1,), (0,)))
    value_part = dot(probs_low, grads, ((1,), (0,)))
    return attended, grad_query, key_part, value_part


def block_rows(frame_rows, ext_rows):
    tiles = frame_rows // TILE
    for step in range(tiles, 0, -1):
        if tiles % step == 0 and 2 * step * TILE * ext_rows <= BLOCK_LIMIT:
            return step * TILE
    return TILE


def listing(tiles, counts, reader, source, frame_tiles, frames):
    reader = jnp.clip(reader, 0, frames - 1)
    masks = []
    for row in range(frame_tiles):
        tile = reader * frame_tiles + row
        mask = jnp.int32(0)
        for slot in range(tiles.shape[0]):
            inside = tiles[slot, tile] - source * frame_tiles
            good = (inside >= 0) & (inside < frame_tiles) & (slot < counts[tile])
            bit = lax.shift_left(jnp.int32(1), jnp.clip(inside, 0, frame_tiles - 1))
            mask = mask | jnp.where(good, bit, 0)
        masks.append(mask)
    return masks


def nth_tiles(masks, frame_tiles, count):
    union = functools.reduce(lambda left, right: left | right, masks)
    seen = jnp.int32(0)
    picked = [[] for _ in range(count)]
    for tile in range(frame_tiles):
        bit = (union >> tile) & 1
        for spot in range(count):
            picked[spot].append((bit == 1) & (seen == spot))
        seen = seen + bit
    return picked


def chunk_spans(width):
    sizes = [LANES] * (width // LANES)
    if width % CHUNK == 0 and width > CHUNK:
        sizes = [LANES] + [CHUNK] * (width // CHUNK - 1) + [CHUNK - LANES]
    return [(sum(sizes[:n]), size) for n, size in enumerate(sizes)]


def relayed(phase, chunk, share, slabs, spans):
    if phase == 0 and chunk + 1 == len(spans):
        return share < 0
    if phase == 0:
        return ((chunk + 1) * share) // slabs > (chunk * share) // slabs
    start, size = spans[chunk]
    total = spans[-1][0] + spans[-1][1]
    return (start + size) * slabs <= total * share


def cuts(chunks, first):
    spans, start, size = [], 0, first
    while start < chunks:
        stop = min(chunks, start + size)
        spans.append((start, stop))
        start, size = stop, size + 1
    return spans


def fused_kernel(
    group, slabs, count, spans, tiles_in, counts_in, q_in, k_in, v_in, g_in,
    early, late,
    own, bias, outgoing, incoming, relay, parts, sums, result,
    send, recv, near, edge_send, edge_recv, relay_send, relay_recv,
    out_send, out_recv, out_near, tiles, counts, list_sem, lead, lead_sem, offer, offered,
    offer_send, offer_recv,
):
    place, slab = lax.axis_index("ulysses"), lax.axis_index("tm")
    side, member = place // group, place % group
    base = side * group
    frames = slabs * FRAMES_SLAB
    frame = slab * FRAMES_SLAB + side
    rows, frame_rows, width = q_in.shape[0], own.shape[1], own.shape[2]
    chunks, widest = len(spans), outgoing.shape[5]
    edge = count * TILE
    frame_tiles = frame_rows // TILE

    turn = 2 * side - 1
    far_slab, onward_slab = slab + turn, slab - turn
    has_far = (far_slab >= 0) & (far_slab < slabs)
    has_onward = (onward_slab >= 0) & (onward_slab < slabs)
    across = {"ulysses": (1 - side) * group + member}
    far = {**across, "tm": jnp.clip(far_slab, 0, slabs - 1)}
    onward = {"tm": jnp.clip(onward_slab, 0, slabs - 1)}
    behind = {"tm": jnp.clip(far_slab, 0, slabs - 1)}
    from_end, from_start = slabs - 1 - slab, slab
    my_share = jnp.where(side == 1, from_end, from_start)
    other_share = jnp.where(side == 1, from_start, from_end)

    def lanes_of(which, start, size):
        return pl.ds(pl.multiple_of(which * width + start, LANES), size)

    def rows_of(which):
        return pl.ds(pl.multiple_of(which * rows, TILE), rows)

    sources = (k_in, v_in, q_in, g_in)
    pieces, nearby, sent = {}, {}, []

    def arrive(number, index):
        for copy in nearby.pop((number, index), []):
            copy.wait()
        for copy in pieces[number, index]:
            copy.wait_recv()

    key_cuts, query_cuts = cuts(chunks, 1), cuts(chunks, max(1, chunks // 2))

    def take(number, index, span):
        start = spans[span[0]][0]
        size = sum(spans[span[1] - 1]) - start
        copy = pltpu.make_async_copy(
            sources[number].at[:, lanes_of(member, start, size)],
            own.at[number, rows_of(member), pl.ds(start, size)], near.at[number, index],
        )
        copy.start()
        nearby[number, index], pieces[number, index] = [copy], []

    def trade(number, index, span):
        start = spans[span[0]][0]
        size = sum(spans[span[1] - 1]) - start
        for step in range(1, group):
            peer = (member + step) % group
            source = sources[number].at[:, lanes_of(peer, start, size)]
            if number < 2 and index == 0:
                source = lead.at[number, step - 1]
            copy = remote(
                source, own.at[number, rows_of(member), pl.ds(start, size)],
                send.at[number, index, step - 1], recv.at[number, index, step - 1],
                {"ulysses": base + peer},
            )
            copy.start()
            pieces[number, index].append(copy)
            sent.append(copy)

    barrier = pltpu.get_barrier_semaphore()
    eager, own_tiles = group == FRAMES_SLAB, rows // TILE

    def opposite(step):
        return {"ulysses": (1 - side) * group + (member + step) % group}

    def hail(device):
        pl.semaphore_signal(barrier, inc=1, device_id=device, device_id_type=MESH)

    @pl.when(has_far)
    def _():
        hail(far)
        hail(behind)

    @pl.when(has_onward)
    def _():
        hail(onward)

    for step in range(1, group):
        hail({"ulysses": base + (member + step) % group})
    for step in range(group if eager else 1):
        hail(opposite(step))

    lists = [
        pltpu.make_async_copy(tiles_in, tiles, list_sem.at[0]),
        pltpu.make_async_copy(counts_in, counts, list_sem.at[1]),
    ]
    for copy in lists:
        copy.start()
    leads = []
    for number in (0, 1):
        for step in range(1, group):
            peer = (member + step) % group
            copy = pltpu.make_async_copy(
                sources[number].at[:, lanes_of(peer, 0, spans[0][1])],
                lead.at[number, step - 1], lead_sem.at[number, step - 1],
            )
            copy.start()
            leads.append(copy)
    for index, span in enumerate(key_cuts):
        for number in (0, 1):
            take(number, index, span)

    for copy in lists:
        copy.wait()
    across_frame, far_frame = frame - turn, frame + turn
    picks = [
        nth_tiles(listing(tiles, counts, reader, frame, frame_tiles, frames), frame_tiles, count)
        for reader in (across_frame, far_frame)
    ]
    def offer_copy(step):
        return remote(
            offer.at[step], offered.at[step], offer_send.at[step], offer_recv.at[step],
            opposite(step),
        )

    def any_of(flags):
        return functools.reduce(lambda left, right: left | right, flags)

    def candidate(step, number, inner):
        start = inner * TILE
        if step:
            return lead[number, step - 1, pl.ds(start, TILE)]
        place_rows = pl.ds(pl.multiple_of(member * rows + start, TILE), TILE)
        return own[number, place_rows, pl.ds(0, spans[0][1])]

    for copy in leads:
        copy.wait()
    if eager:
        for number in (0, 1):
            for copy in nearby.pop((number, 0)):
                copy.wait()
            for step in range(group):
                for spot in range(count):
                    chosen = candidate(step, number, 0)
                    for inner in range(1, own_tiles):
                        flag = any_of([
                            (member == m) & picks[0][spot][m * own_tiles + inner]
                            for m in range(group)
                        ])
                        chosen = jnp.where(flag, candidate(step, number, inner), chosen)
                    offer[step, number, pl.ds(spot * TILE, TILE)] = chosen
    pl.semaphore_wait(
        barrier, (2 * group - 1 if eager else group) + jnp.where(has_far, 2, 0) + jnp.where(has_onward, 1, 0)
    )
    if eager:
        for step in range(group):
            offer_copy(step).start()
    for number in (0, 1):
        trade(number, 0, key_cuts[0])
    for index, span in enumerate(key_cuts[1:]):
        for number in (0, 1):
            trade(number, index + 1, span)

    def lot(ref, chunk):
        return ref if spans[chunk][1] == widest else ref.at[:, :, pl.ds(0, spans[chunk][1])]

    def edge_copy(phase, way, chunk, device):
        return remote(
            lot(outgoing.at[phase, way, chunk], chunk), lot(incoming.at[phase, way, chunk], chunk),
            edge_send.at[phase, way, chunk], edge_recv.at[phase, way, chunk], device,
        )

    def relay_in(phase, chunk):
        return remote(
            lot(outgoing.at[phase, 1, chunk], chunk), lot(relay.at[phase, chunk], chunk),
            edge_send.at[phase, 1, chunk], relay_recv.at[phase, chunk], across,
        )

    def relay_out(phase, chunk):
        return remote(
            lot(relay.at[phase, chunk], chunk), lot(incoming.at[phase, 1, chunk], chunk),
            relay_send.at[phase, chunk], edge_recv.at[phase, 1, chunk], onward,
        )

    def passes(phase, chunk):
        return has_onward & relayed(phase, chunk, other_share, slabs, spans)

    def send_across(phase, chunk):
        if eager and (phase, chunk) == (0, 0):
            return
        edge_copy(phase, 0, chunk, across).start()

    def send_far(phase, chunk):
        around = relayed(phase, chunk, my_share, slabs, spans)

        @pl.when(has_far & jnp.logical_not(around))
        def _():
            edge_copy(phase, 1, chunk, far).start()

        @pl.when(has_far & around)
        def _():
            relay_in(phase, chunk).start()

    def pass_on(phase, chunk):
        @pl.when(passes(phase, chunk))
        def _():
            relay_in(phase, chunk).wait_recv()
            relay_out(phase, chunk).start()

    def accept():
        size = spans[0][1]
        for step in range(group):
            offer_copy(step).wait_recv()
        for spot in range(count):
            rows_here = pl.ds(spot * TILE, TILE)
            for number in (0, 1):
                chosen = offered[0, number, rows_here]
                for step in range(1, group):
                    flag = any_of([
                        ((member - step + group) % group == tile // own_tiles) & across_picks[spot][tile]
                        for tile in range(frame_tiles)
                    ])
                    chosen = jnp.where(flag, offered[step, number, rows_here], chosen)
                incoming[0, 0, 0, number, rows_here, pl.ds(0, size)] = chosen

    def receive_edges(phase, chunk):
        if eager and (phase, chunk) == (0, 0):
            accept()
        else:
            edge_copy(phase, 0, chunk, across).wait_recv()

        @pl.when(has_far)
        def _():
            edge_copy(phase, 1, chunk, far).wait_recv()

    def settle_edges(phase, chunk):
        if eager and (phase, chunk) == (0, 0):
            for step in range(group):
                offer_copy(step).wait_send()
        else:
            edge_copy(phase, 0, chunk, across).wait_send()

        @pl.when(has_far)
        def _():
            edge_copy(phase, 1, chunk, far).wait_send()

        @pl.when(passes(phase, chunk))
        def _():
            relay_out(phase, chunk).wait_send()

    for index, span in enumerate(key_cuts):
        for number in (0, 1):
            arrive(number, index)
        for chunk in range(*span):
            columns = pl.ds(*spans[chunk])
            size = spans[chunk][1]
            for number in (0, 1):
                for way in range(2):
                    for spot in range(count):
                        chosen = own[number, pl.ds(0, TILE), columns]
                        for tile in range(1, frame_tiles):
                            here = own[number, pl.ds(tile * TILE, TILE), columns]
                            chosen = jnp.where(picks[way][spot][tile], here, chosen)
                        outgoing[0, way, chunk, number, pl.ds(spot * TILE, TILE), pl.ds(0, size)] = chosen
            send_far(0, chunk)
            send_across(0, chunk)
        if index == 0:
            for piece, part in enumerate(query_cuts):
                for number in (2, 3):
                    take(number, piece, part)
                    trade(number, piece, part)

    @pl.when(jnp.logical_not(has_far))
    def _():
        for phase in range(2):
            for chunk in range(chunks):
                incoming[phase, 1, chunk] = jnp.zeros((2, edge, widest), BF16)

    blocks, step_rows = bias.shape[0], bias.shape[2]
    across_rows = listing(tiles, counts, frame, across_frame, frame_tiles, frames)
    across_picks = nth_tiles(across_rows, frame_tiles, count)
    own_masks = listing(tiles, counts, frame, frame, frame_tiles, frames)
    far_rows = listing(tiles, counts, frame, far_frame, frame_tiles, frames)

    def edge_hits(masks):
        picked = nth_tiles(masks, frame_tiles, count)
        hits = []
        for spot in range(count):
            bit = jnp.int32(0)
            for tile in range(frame_tiles):
                bit = bit + jnp.where(picked[spot][tile], 1 << tile, 0)
            hits.append([(mask & bit) != 0 for mask in masks])
        return hits

    hits = edge_hits(across_rows)
    hits += [[((mask >> tile) & 1) == 1 for mask in own_masks] for tile in range(frame_tiles)]
    hits += edge_hits(far_rows)
    block_tiles = step_rows // TILE
    inner = lax.broadcasted_iota(jnp.int32, (1, step_rows), 1) // TILE
    for number, row in enumerate(hits):
        for block in range(blocks):
            line = jnp.full((1, step_rows), DEAD, F32)
            for spot in range(block_tiles):
                level = jnp.where(row[block * block_tiles + spot], 0.0, DEAD)
                line = jnp.where(inner == spot, level, line)
            bias[block, pl.ds(number, 1)] = line

    leaving = {}

    def share(phase, chunk):
        start, size = spans[chunk]
        target, columns = (early, late)[phase], pl.ds(start, size)
        there = lanes_of(member, start, size)
        copies = [pltpu.make_async_copy(
            result.at[phase, :, rows_of(member), columns], target.at[:, :, there],
            out_near.at[phase, chunk],
        )]
        for step in range(1, group):
            peer = (member + step) % group
            copies.append(remote(
                result.at[phase, :, rows_of(peer), columns], target.at[:, :, there],
                out_send.at[phase, chunk, step - 1], out_recv.at[phase, chunk, step - 1],
                {"ulysses": base + peer},
            ))
        for copy in copies:
            copy.start()
        leaving[phase, chunk] = copies

    def attend(chunk):
        @pl.loop(0, spans[chunk][1] // LANES)
        def _(pair):
            inside = pl.ds(pl.multiple_of(pair * LANES, LANES), LANES)
            lanes = pl.ds(pl.multiple_of(spans[chunk][0] + pair * LANES, LANES), LANES)

            def stacked(number):
                return jnp.concatenate([
                    incoming[0, 0, chunk, number, :, inside], own[number, :, lanes],
                    incoming[0, 1, chunk, number, :, inside],
                ])

            for block in range(blocks):
                span = pl.ds(block * step_rows, step_rows)
                out, grad_rows, key_part, value_part = heads_math(
                    own[2, span, lanes], own[3, span, lanes], stacked(0), stacked(1), bias[block],
                )
                result[0, 0, span, lanes] = out
                result[0, 1, span, lanes] = grad_rows
                for number, part in enumerate((key_part, value_part)):
                    if block:
                        part = part + sums[number]
                    if block + 1 < blocks:
                        sums[number] = part
                        continue
                    outgoing[1, 0, chunk, number, :, inside] = part[:edge].astype(BF16)
                    parts[number, :, lanes] = part[edge : edge + frame_rows]
                    outgoing[1, 1, chunk, number, :, inside] = part[edge + frame_rows :].astype(BF16)

    for chunk in range(chunks + LAG):
        if chunk < chunks:
            pass_on(0, chunk)
        ready = chunk - LAG
        if ready < 0:
            continue
        for piece, part in enumerate(query_cuts):
            if part[0] == ready:
                for number in (2, 3):
                    arrive(number, piece)
        receive_edges(0, ready)
        attend(ready)
        send_far(1, ready)
        if ready >= HOLD:
            send_across(1, ready - HOLD)
        share(0, ready)

    for chunk in range(max(0, chunks - HOLD), chunks):
        send_across(1, chunk)
    for copy in sent:
        copy.wait_send()
    for chunk in range(chunks):
        settle_edges(0, chunk)

    def gather(chunk):
        columns, size = pl.ds(*spans[chunk]), spans[chunk][1]
        for number in range(2):
            for tile in range(frame_tiles):
                span = pl.ds(tile * TILE, TILE)
                total = parts[number, span, columns]
                for way in range(2):
                    for spot in range(count):
                        part = incoming[1, way, chunk, number, pl.ds(spot * TILE, TILE), pl.ds(0, size)]
                        total = total + jnp.where(picks[way][spot][tile], part.astype(F32), 0.0)
                result[1, number, span, columns] = total.astype(BF16)
        share(1, chunk)

    for chunk in range(chunks + LAG):
        if chunk < chunks:
            pass_on(1, chunk)
        ready = chunk - LAG
        if ready < 0:
            continue
        for copy in leaving.pop((0, ready)):
            copy.wait()
        if ready:
            settle_edges(1, ready - 1)
        if ready > 1:
            for copy in leaving.pop((1, ready - 2)):
                copy.wait()
        receive_edges(1, ready)
        gather(ready)

    settle_edges(1, chunks - 1)
    for copies in leaving.values():
        for copy in copies:
            copy.wait()


def flush_kernel(early, late, *refs):
    sems = refs[4]
    copies = [
        pltpu.make_async_copy((early, late)[n // 2].at[n % 2], refs[n], sems.at[n])
        for n in range(4)
    ]
    for copy in copies:
        copy.start()
    for copy in copies:
        copy.wait()


def per_device(slabs, group, queries, key_vectors, value_vectors, grad_out, key_tiles, tile_counts):
    rows, columns = queries.shape
    width = columns // group
    frame_rows = rows * group
    frame_tiles = frame_rows // TILE
    count = max(1, frame_tiles // 8)
    edge = count * TILE
    ext_rows = frame_rows + 2 * edge
    spans = chunk_spans(width)
    chunks, chunk_width = len(spans), max(size for _, size in spans)
    step_rows = block_rows(frame_rows, ext_rows)
    blocks = frame_rows // step_rows
    key_pieces, query_pieces = len(cuts(chunks, 1)), len(cuts(chunks, max(1, chunks // 2)))
    most = max(key_pieces, query_pieces)

    vmem = pl.BlockSpec(memory_space=pltpu.VMEM)
    hbm = pl.BlockSpec(memory_space=pltpu.HBM)
    dma = pltpu.SemaphoreType.DMA
    arguments = [
        pltpu.with_memory_space_constraint(value, pltpu.HBM)
        for value in (key_tiles.T, tile_counts, queries, key_vectors, value_vectors, grad_out)
    ]
    results = pl.pallas_call(
        functools.partial(fused_kernel, group, slabs, count, spans),
        out_shape=(jax.ShapeDtypeStruct((2, rows, columns), BF16),) * 2,
        in_specs=[hbm] * 6,
        out_specs=(vmem,) * 2,
        scratch_shapes=[
            pltpu.VMEM((4, frame_rows, width), BF16),
            pltpu.VMEM((blocks, ext_rows // TILE, step_rows), F32),
            pltpu.VMEM((2, 2, chunks, 2, edge, chunk_width), BF16),
            pltpu.VMEM((2, 2, chunks, 2, edge, chunk_width), BF16),
            pltpu.VMEM((2, chunks, 2, edge, chunk_width), BF16),
            pltpu.VMEM((2, frame_rows, width), F32),
            pltpu.VMEM((2, ext_rows if blocks > 1 else TILE, LANES), F32),
            pltpu.VMEM((2, 2, frame_rows, width), BF16),
            dma((4, most, group - 1)), dma((4, most, group - 1)), dma((4, most)),
            dma((2, 2, chunks)), dma((2, 2, chunks)), dma((2, chunks)), dma((2, chunks)),
            dma((2, chunks, group - 1)), dma((2, chunks, group - 1)), dma((2, chunks)),
            pltpu.SMEM(key_tiles.T.shape, jnp.int32), pltpu.SMEM(tile_counts.shape, jnp.int32), dma((2,)),
            pltpu.VMEM((2, group - 1, rows, spans[0][1]), BF16), dma((2, group - 1)),
            pltpu.VMEM((group, 2, edge, spans[0][1]), BF16), pltpu.VMEM((group, 2, edge, spans[0][1]), BF16),
            dma((group,)), dma((group,)),
        ],
        compiler_params=pltpu.CompilerParams(
            collective_id=0, has_side_effects=True, vmem_limit_bytes=32 << 20
        ),
        name="frame_attention",
    )(*arguments)
    return pl.pallas_call(
        flush_kernel,
        out_shape=(jax.ShapeDtypeStruct((rows, columns), BF16),) * 4,
        in_specs=[vmem] * 2,
        out_specs=(hbm,) * 4,
        scratch_shapes=[dma((4,))],
        compiler_params=pltpu.CompilerParams(vmem_limit_bytes=16 << 20),
        name="flush_results",
    )(*results)


def solution(mesh):
    tokens = P(("clips", "tm", "ulysses"), None)
    group = mesh.shape["ulysses"] // FRAMES_SLAB
    return jax.shard_map(
        functools.partial(per_device, mesh.shape["tm"], group),
        mesh=mesh,
        in_specs=(tokens, tokens, tokens, tokens, P("clips", None), P("clips")),
        out_specs=(tokens,) * 4,
        check_vma=False,
    )
```
